256 devices in a mesh: seq: 128 (over x, y, z), head: 2 (over core).
Axes of the slice: x: 4, y: 4, z: 8, core: 2. Of those that a mesh axis runs over, the one named last changes fastest.
Arguments:
- tiles: bfloat16 [16384, 768], P('seq', 'head'), may hold values from -6 to 6
- ln_gain: float32 [768], replicated, may hold values from 0.25 to 1.75
- w_qkv: bfloat16 [768, 3, 768], P(None, None, 'head'), as said below
- w_out: bfloat16 [768, 768], P('head'), may hold values from -0.21875 to 0.21875
- tile_source: int32 [16384], P('seq'), may hold values from 0 to 16383, as said below
- tissue_count: int32 [128], P('seq'), may hold values from 64 to 128
Outputs:
- encoded: bfloat16 [16384, 768], P('seq', 'head')
The draws below stay inside these ranges and needn't reach their ends.
Inputs may be any that keep to these rules, and one draw needn't show every extreme that they name: `tile_source`: A permutation of the 16384 rows; exactly one tile goes to Hilbert block d from each encoder block s, namely row s * 128 + d; within block d these 128 tiles come in any order. `w_qkv`: projection weights; the query third may be larger than the key and value thirds.
All inputs are finite; a program needn't handle non-finite values.
Results may differ from the reference program's by a relative error of at most 0.0095.
The reference program's roundings to bfloat16 on the way (of `relaid`, `normed` and `attended`) count: a program that leaves them out, or rounds other values in their place, can miss the bound.
Values may be sent and summed in bfloat16 or wider, within the bound.
A program may use at most 64 MiB of HBM per device.

```python
import math
from functools import reduce
import jax
import jax.numpy as jnp
from jax import lax

D = 768
HEADS = 12
HEAD_DIM = 64
TILES_PER_BLOCK = 128
SPAN_SHORT = 4
MIDDLE_SPAN = 16
MIDDLE_DILATION = 4
WHOLE_DILATION = 16
BLOCKS = 128
TOKENS = 16384


def draw_tile_source(key, part):
    per_peer = TILES_PER_BLOCK // BLOCKS
    slot_index = jnp.arange(TILES_PER_BLOCK, dtype=jnp.int32)
    owner = slot_index // per_peer
    within = slot_index % per_peer
    sub_keys = jax.random.split(key, BLOCKS)

    def one_block(target, sub_key):
        sources = owner * TILES_PER_BLOCK + target * per_peer + within
        return jax.random.permutation(sub_key, sources)
    result = jax.vmap(one_block)(jnp.arange(BLOCKS, dtype=jnp.int32), sub_keys)
    return result.reshape(BLOCKS * TILES_PER_BLOCK).astype(jnp.int32)


def draw_tissue_count(key, part):
    first_key, second_key = jax.random.split(key)
    counts = jax.random.randint(first_key, (BLOCKS,), TILES_PER_BLOCK // 2, TILES_PER_BLOCK + 1)
    ordering = jax.random.permutation(second_key, BLOCKS)
    counts = counts.at[ordering[0]].set(TILES_PER_BLOCK).at[ordering[1]].set(TILES_PER_BLOCK // 2)
    return counts.astype(jnp.int32)


def draw_w_qkv(key, part):
    base_key = jax.random.fold_in(key, 0)
    base = jax.random.truncated_normal(base_key, -4.0, 4.0, (D, 3, D), jnp.float32) / math.sqrt(D)
    head_scale = jnp.full((HEADS,), 3.0, jnp.float32)
    query_scale = jnp.repeat(head_scale, HEAD_DIM)
    factor = jnp.stack([query_scale, jnp.ones((D,), jnp.float32), jnp.ones((D,), jnp.float32)], 0)
    return (base * factor[None]).astype(jnp.bfloat16)


def block_scale(stream_key, shape, cuts, smallest, top_value):
    def one(axis_at, shards_of):
        draws = jax.random.uniform(jax.random.fold_in(jax.random.fold_in(stream_key, 6), axis_at), (shards_of,), jnp.float32, smallest / len(cuts), top_value / len(cuts))
        return jnp.repeat(jnp.exp(draws), shape[axis_at] // shards_of).reshape((-1,) + (1,) * (len(shape) - axis_at - 1))

    gain = one(*cuts[0])
    for cut in cuts[1:]:
        gain = gain * one(*cut)
    return gain


def centred(rng, dims, deviation, limit, cuts=(), kind=jnp.bfloat16):
    gain = block_scale(rng, dims, cuts, -0.22, 0.18) if cuts else 1.0
    array = jax.random.normal(rng, dims, jnp.float32) * deviation * gain
    return jnp.minimum(jnp.maximum(array, -limit), limit).astype(kind)


def setup_inputs(seed: int = 0) -> dict:
    seeds = jax.random.split(jax.random.key(seed), 7)
    return {
        "tiles": centred(seeds[0], (TOKENS, D), 1.0, 6.0, ((0, 128), (1, 2))),
        "ln_gain": jnp.clip(1.0 + 0.15 * jax.random.normal(seeds[1], (D,), jnp.float32), 0.25, 1.75),
        "w_qkv": draw_w_qkv(jax.random.fold_in(seeds[6], 71), 0),
        "w_out": centred(seeds[3], (D, D), D ** -0.5, 0.21875, ((0, 2),)),
        "tile_source": draw_tile_source(jax.random.fold_in(seeds[6], 71), 0),
        "tissue_count": draw_tissue_count(jax.random.fold_in(seeds[6], 71), 0),
    }


masked_score = -1e+30

def apply_dilation(key_matrix, value_matrix, row_active_mask, stride):
    kept_rows = TOKENS // stride
    offsets = jnp.arange(HEADS, dtype=jnp.int32) % stride
    selector = jnp.broadcast_to(offsets[None, None, :, None], (kept_rows, 1, HEADS, HEAD_DIM))
    picked_keys = jnp.take_along_axis(key_matrix.reshape(kept_rows, stride, HEADS, HEAD_DIM), selector, axis=1)[:, 0]
    picked_values = jnp.take_along_axis(value_matrix.reshape(kept_rows, stride, HEADS, HEAD_DIM), selector, axis=1)[:, 0]
    picked_live = row_active_mask.reshape(kept_rows, stride)[:, offsets]
    return (picked_keys, picked_values, picked_live)

def branch(queries, key_matrix, value_matrix, key_live):
    scores = jnp.einsum('qhd,khd->hqk', queries.astype(jnp.float32), key_matrix.astype(jnp.float32)) * HEAD_DIM ** (-0.5)
    scores = jnp.where(key_live.T[:, None, :] > 0.5, scores, masked_score)
    row_max = lax.optimization_barrier(jnp.max(scores, axis=-1))
    weights = jnp.exp(scores - row_max[..., None])
    row_sum = lax.optimization_barrier(jnp.sum(weights, axis=-1))
    rounded = lax.optimization_barrier(weights.astype(jnp.bfloat16)).astype(jnp.float32)
    mixed = jnp.einsum('hqk,khd->qhd', rounded, value_matrix.astype(jnp.float32))
    return (row_max, row_sum, mixed)

def reference(tiles, ln_gain, w_qkv, w_out, tile_source, tissue_count):
    relaid = tiles[tile_source].astype(jnp.float32)
    row_mean = lax.optimization_barrier(jnp.mean(relaid, axis=-1, keepdims=True))
    centered = relaid - row_mean
    row_var = lax.optimization_barrier(jnp.mean(centered * centered, axis=-1, keepdims=True))
    normed = (centered * lax.rsqrt(row_var + 1e-05) * ln_gain).astype(jnp.bfloat16)
    packed = jnp.dot(normed, w_qkv.reshape(D, 3 * D), preferred_element_type=jnp.float32).astype(jnp.bfloat16)
    packed = lax.optimization_barrier(packed).reshape(TOKENS, 3, HEADS, HEAD_DIM)
    queries, key_matrix, value_matrix = (packed[:, 0], packed[:, 1], packed[:, 2])
    position = jnp.arange(TOKENS, dtype=jnp.int32)
    row_active_mask = (position % TILES_PER_BLOCK < tissue_count[position // TILES_PER_BLOCK]).astype(jnp.float32)
    live_all = jnp.broadcast_to(row_active_mask[:, None], (TOKENS, HEADS))
    middle_branch = apply_dilation(key_matrix, value_matrix, row_active_mask, MIDDLE_DILATION)
    faraway_part = apply_dilation(key_matrix, value_matrix, row_active_mask, WHOLE_DILATION)
    short_len = SPAN_SHORT * TILES_PER_BLOCK
    middle_length = MIDDLE_SPAN * TILES_PER_BLOCK // MIDDLE_DILATION

    def one_block(block_index):
        queries_here = lax.dynamic_slice_in_dim(queries, block_index * TILES_PER_BLOCK, TILES_PER_BLOCK, 0)
        short_start = block_index // SPAN_SHORT * short_len
        middle_start = block_index // MIDDLE_SPAN * middle_length
        results = [branch(queries_here, *[lax.dynamic_slice_in_dim(member, short_start, short_len, 0) for member in (key_matrix, value_matrix, live_all)]), branch(queries_here, *[lax.dynamic_slice_in_dim(member, middle_start, middle_length, 0) for member in middle_branch]), branch(queries_here, *faraway_part)]
        overall = reduce(jnp.maximum, [entry[0] for entry in results])
        numerator = sum((jnp.exp(entry[0] - overall).T[:, :, None] * entry[2] for entry in results))
        denominator = sum((jnp.exp(entry[0] - overall) * entry[1] for entry in results))
        outcome = numerator / denominator.T[:, :, None]
        live_here = lax.dynamic_slice_in_dim(row_active_mask, block_index * TILES_PER_BLOCK, TILES_PER_BLOCK, 0)
        return (outcome * live_here[:, None, None]).astype(jnp.bfloat16).reshape(TILES_PER_BLOCK, D)
    attended = lax.map(one_block, jnp.arange(BLOCKS, dtype=jnp.int32)).reshape(TOKENS, D)
    return jnp.dot(attended, w_out, preferred_element_type=jnp.float32).astype(jnp.bfloat16)
```

```python
import jax
import jax.numpy as jnp
from jax import lax
from jax.experimental import pallas as pl
from jax.experimental.pallas import tpu as pltpu
from jax.sharding import PartitionSpec as P

D = 768
HALF = 384
ROWS = 128
NX, NY, NZ = 4, 4, 8
SEG = 4
LONG = SEG * 8
NEG = -1e30
F32 = jnp.float32
BF16 = jnp.bfloat16
MESH = pl.DeviceIdType.MESH
PLAIN = (((1,), (0,)), ((), ()))
MINOR = (((1,), (1,)), ((), ()))
MAJOR = (((0,), (0,)), ((), ()))


def iota(shape, dim):
    return lax.broadcasted_iota(jnp.int32, shape, dim)


def dot(a, b, dims):
    return lax.dot_general(a, b, dims, preferred_element_type=F32)


def kernel(
    tiles, gain_in, w_qkv, w_out_in, src_in, cnt_in,
    out,
    w_v, w_out, gain, src, cnt, A, C, DD, E, SRC, R, PM, SEL,
    KS, VS, MKS, GF, HM, QA, M, L, O, AS, AT, PO, PI,
    w_sem, loc_sem,
    xs_s, xs_r, zs_s, zs_r, ps_s, ps_r, src_s, src_r,
    gf_s, gf_r, hm_s, hm_r, at_s, at_r, o_s, o_r,
):
    seq = lax.axis_index("seq")
    core = lax.axis_index("head")
    x, y, z = seq // (NY * NZ), (seq // NZ) % NY, seq % NZ
    zh, zj = z // SEG, z % SEG
    place = zj + zh * (SEG - 1 - 2 * zj)
    pair = (place + 1) // 2
    first_head = 6 * core + 2 * pair
    sibling = {"head": 1 - core}
    pending = []

    def at(px, py, pz):
        return {"seq": (px * NY + py) * NZ + pz}

    def remote(source, target, s_sem, r_sem, device):
        return pltpu.make_async_remote_copy(
            src_ref=source, dst_ref=target, send_sem=s_sem, recv_sem=r_sem,
            device_id=device, device_id_type=MESH,
        )

    def send(source, target, s_sem, r_sem, device):
        copy = remote(source, target, s_sem, r_sem, device)
        copy.start()
        pending.append(copy)
        return copy

    lanes = pl.ds(pl.multiple_of(pair * ROWS, ROWS), ROWS)
    weights = [
        pltpu.make_async_copy(w_qkv.at[t, :, lanes], w_v.at[:, t * ROWS : (t + 1) * ROWS], w_sem.at[t])
        for t in range(3)
    ]
    weights += [pltpu.make_async_copy(w_out_in, w_out, w_sem.at[3])]
    weights += [pltpu.make_async_copy(gain_in, gain, w_sem.at[4])]
    small = [
        pltpu.make_async_copy(src_in, src, loc_sem.at[1]),
        pltpu.make_async_copy(cnt_in, cnt, loc_sem.at[2]),
    ]
    own_a = pltpu.make_async_copy(tiles.at[x], A.at[0], loc_sem.at[0])
    barrier = pltpu.get_barrier_semaphore()
    peers = [at((x + k) % NX, y, z) for k in range(1, NX)] + [sibling]
    plane = [(o // NZ, o % NZ) for o in range(1, NY * NZ)]
    peers += [at(x, (y + dy) % NY, (z + dz) % NZ) for dy, dz in plane]
    for peer in peers:
        pl.semaphore_signal(barrier, inc=1, device_id=peer, device_id_type=MESH)
    for copy in small + weights + [own_a]:
        copy.start()
    for copy in small:
        copy.wait()
    own_count = cnt[0]
    rows8 = iota((8, ROWS), 0)
    tag = jnp.where(rows8 == 0, src[...] // ROWS, own_count)
    SRC[zj] = tag.astype(F32)
    pl.semaphore_wait(barrier, len(peers))

    in_x = [
        send(tiles.at[(x + k) % NX], A.at[k], xs_s.at[k], xs_r.at[k], at((x + k) % NX, y, z))
        for k in range(1, NX)
    ]
    in_src = [
        send(SRC.at[zj], SRC.at[zj], src_s.at[t], src_r.at[t], at(x, y, SEG * zh + (zj + t) % SEG))
        for t in range(1, SEG)
    ]
    own_a.wait()
    row, col = iota((ROWS, ROWS), 0), iota((ROWS, ROWS), 1)
    turn = (((row >> 2) & 3) * 32 + (row >> 4) * 4 + (row & 3) == col).astype(BF16)
    for copy in in_x:
        copy.wait_recv()
    turned = dot(turn, A[...].reshape(ROWS, HALF), PLAIN)
    C[...] = turned.astype(BF16).reshape(2 * NY, 16, HALF)

    in_z = [[] for _ in range(NY)]
    for dy, dz in plane:
        yt, zt = (y + dy) % NY, (z + dz) % NZ
        o = dy * NZ + dz
        in_z[dy].append(
            send(C.at[2 * yt + zt // SEG], DD.at[dy, dz], zs_s.at[o], zs_r.at[o], at(x, yt, zt))
        )
    DD[0, 0] = C[2 * y + zh]

    for copy in in_src:
        copy.wait_recv()
    lane512 = iota((1, 512), 1)
    from_x, from_y = (x + NX - ((lane512 >> 2) & 3)) & 3, (y + NY - (lane512 >> 7)) & 3
    from_z = (z + NZ - ((lane512 >> 4) & 7)) & 7
    code = (((from_x * NY + from_y) * NZ + from_z) * SEG + (lane512 & 3)).astype(F32)
    place_iota = iota((ROWS, ROWS), 0).astype(F32)
    for b in range(SEG):
        block = SRC[b]
        wanted = jnp.transpose(block)[:, 0:1] * SEG + b
        PM[b * ROWS : (b + 1) * ROWS] = (wanted == code).astype(BF16)
        alive = place_iota < block[1:2]
        MKS[b * ROWS : (b + 1) * ROWS] = jnp.where(alive, 0.0, NEG).astype(BF16)
        AS[b] = (iota((ROWS, ROWS), 1).astype(F32) < block[1:2]).astype(BF16)
        GF[0, 0, 0, 64 + b : 65 + b] = block[1:2].astype(BF16)
        QA[b, 0:ROWS, ROWS:] = (col == 0).astype(BF16)
        QA[b, ROWS:, ROWS:] = (col == 1).astype(BF16)
        M[b] = jnp.full((8, 256), NEG, F32)
        L[b] = jnp.zeros((8, 256), F32)
        O[b] = jnp.zeros((ROWS, 256), F32)
    GF[0, 0, 0, 68:72] = jnp.zeros((4, ROWS), BF16)
    out_row, from_row = iota((160, 512), 0), iota((160, 512), 1)
    for h in range(2):
        head = first_head + h
        mid = (out_row >> 5) * ROWS + (out_row & 31) * 4 + head % 4
        far_row = out_row - ROWS
        far = (far_row >> 3) * ROWS + (far_row & 7) * 16 + head
        SEL[h] = (jnp.where(out_row < ROWS, mid, far) == from_row).astype(BF16)
    for copy in weights:
        copy.wait()

    gain_mine = jnp.concatenate([gain[pl.ds(3 * core + i, 1)] for i in range(3)], axis=1)
    gain_other = jnp.concatenate([gain[pl.ds(3 - 3 * core + i, 1)] for i in range(3)], axis=1)
    w_mine = w_v[pl.ds(pl.multiple_of(core * HALF, HALF), HALF)]
    w_other = w_v[pl.ds(pl.multiple_of((1 - core) * HALF, HALF), HALF)]
    in_p = []

    def project(c):
        a = DD[c].reshape(ROWS, HALF).astype(F32)
        b = E[c].reshape(ROWS, HALF).astype(F32)
        mean = (jnp.sum(a, 1, keepdims=True) + jnp.sum(b, 1, keepdims=True)) / D
        a, b = a - mean, b - mean
        var = (jnp.sum(a * a, 1, keepdims=True) + jnp.sum(b * b, 1, keepdims=True)) / D
        scale = lax.rsqrt(var + 1e-05)
        a = (a * scale * gain_mine).astype(BF16)
        b = (b * scale * gain_other).astype(BF16)
        R[c * ROWS : (c + 1) * ROWS] = (dot(a, w_mine, PLAIN) + dot(b, w_other, PLAIN)).astype(BF16)

    for c in range(NY):
        for copy in in_z[c]:
            copy.wait_recv()
        in_p.append(send(DD.at[c], E.at[c], ps_s.at[c], ps_r.at[c], sibling))
        if c:
            in_p[c - 1].wait_recv()
            project(c - 1)
    in_p[NY - 1].wait_recv()
    project(NY - 1)

    qkv = dot(PM[...], R[...], PLAIN)
    kv = qkv[:, ROWS:].astype(BF16)
    low = (iota((1, 2 * ROWS), 1) & 127) < 64
    picked = jnp.where(low, dot(SEL[0], kv, PLAIN), dot(SEL[1], kv, PLAIN)).astype(BF16)
    HM[0, 0, 0:ROWS] = picked[0:ROWS, 0:ROWS]
    HM[0, 0, ROWS:] = picked[0:ROWS, ROWS:]
    GF[0, 0, 0, 0:LONG] = picked[ROWS:, 0:ROWS]
    GF[0, 0, 0, LONG : 2 * LONG] = picked[ROWS:, ROWS:]

    def z_of(f):
        return z + f * (NZ - 1 - 2 * z)

    y_pair = y + 1 - 2 * (y % 2)
    in_m = []
    for yy, f in ((1, 0), (0, 1), (1, 1)):
        in_m.append(
            send(
                HM.at[0, 0], HM.at[yy, f], hm_s.at[2 * yy + f], hm_r.at[2 * yy + f],
                at(x, y_pair if yy else y, z_of(f)),
            )
        )
    in_g = [[] for _ in range(NX)]
    for dx in (2, 1, 3, 0):
        for dy in (2, 1, 3, 0):
            for f in (1, 0):
                if dx or dy or f:
                    o = (dx * NY + dy) * 2 + f
                    in_g[dx].append(
                        send(
                            GF.at[0, 0, 0], GF.at[dx, dy, f], gf_s.at[o], gf_r.at[o],
                            at((x + dx) % NX, (y + dy) % NY, z_of(f)),
                        )
                    )
    KS[...] = kv[:, 0:ROWS]
    VS[...] = kv[:, ROWS:]
    q32 = qkv[:, 0:ROWS].astype(BF16).astype(F32) * 0.125
    for b in range(SEG):
        q_b = q32[b * ROWS : (b + 1) * ROWS]
        QA[b, 0:ROWS, 0:ROWS] = jnp.where(col < 64, q_b, 0.0).astype(BF16)
        QA[b, ROWS:, 0:ROWS] = jnp.where(col < 64, 0.0, q_b).astype(BF16)

    def absorb(keys, values, masks):
        keys = jnp.concatenate([keys, masks], axis=1)
        for b in range(SEG):
            scores = dot(keys, QA[b], MINOR)
            old = M[b][0:1]
            new = jnp.maximum(old, jnp.max(scores, axis=0, keepdims=True))
            weight = jnp.exp(scores - new)
            rescale = jnp.exp(old - new)
            total = L[b][0:1] * rescale + jnp.sum(weight, axis=0, keepdims=True)
            O[b] = O[b] * rescale + dot(values, weight.astype(BF16), MAJOR)
            M[b] = jnp.broadcast_to(new, (8, 256))
            L[b] = jnp.broadcast_to(total, (8, 256))

    def mask(n, counts, segment_rows, stride):
        r, c = iota((n, counts.shape[0]), 0), iota((n, counts.shape[0]), 1)
        per_block = segment_rows // SEG
        owner = ((r // segment_rows) * 8 + (r % segment_rows) // per_block == c).astype(BF16)
        position = (iota((n, ROWS), 0) % per_block) * stride
        position = position + (first_head + jnp.minimum(iota((n, ROWS), 1), 1)) % stride
        alive = position.astype(F32) < dot(owner, counts, PLAIN)
        return jnp.where(alive, 0.0, NEG).astype(BF16)

    absorb(KS[...], VS[...], MKS[...])

    for dx in (0, 1, 3, 2):
        for copy in in_g[dx]:
            copy.wait_recv()
        if dx == 0:
            for copy in in_m:
                copy.wait_recv()
            near = [GF[0, 0, 0, 64:72], GF[0, 0, 1, 64:72]]
            slot = NY - 1 - 2 * (y % 2)
            near += [GF[0, slot, 0, 64:72], GF[0, slot, 1, 64:72]]
            near = jnp.concatenate([part.astype(F32) for part in near], axis=0).astype(BF16)
            absorb(
                HM[:, :, 0:ROWS].reshape(512, ROWS),
                HM[:, :, ROWS:].reshape(512, ROWS),
                mask(512, near, ROWS, 4),
            )
        tags = GF[dx, :, :, 64:72].astype(F32).reshape(64, ROWS).astype(BF16)
        absorb(
            GF[dx, :, :, 0:LONG].reshape(256, ROWS),
            GF[dx, :, :, LONG : 2 * LONG].reshape(256, ROWS),
            mask(256, tags, LONG, 16),
        )

    for b in range(SEG):
        halves = []
        for h in range(2):
            cols = slice(h * ROWS, (h + 1) * ROWS)
            halves.append(O[b][h * 64 : (h + 1) * 64, cols] / L[b][0:1, cols])
        AS[b] = (jnp.concatenate(halves, axis=0) * AS[b].astype(F32)).astype(BF16)
    AT[pair] = AS[zj]
    backs = []
    for target in range(SEG):
        block = target + zh * (SEG - 1 - 2 * target)
        copy = remote(
            AS.at[block], AT.at[pair], at_s.at[target], at_r.at[pair], at(x, y, SEG * zh + block)
        )
        senders = [p for p in (0, 3) if p != target] + {0: [1], 3: [2]}.get(target, [])
        here = place == senders[0]
        for p in senders[1:]:
            here = here | (place == p)
        backs.append((copy, here))
        pl.when(here)(copy.start)
    for g in range(3):
        arrival = remote(AS.at[0], AT.at[g], at_s.at[0], at_r.at[g], sibling)
        pl.when(pair != g)(arrival.wait_recv)
    attended = AT[...].reshape(HALF, ROWS)
    mine = pl.ds(pl.multiple_of(core * HALF, HALF), HALF)
    other = pl.ds(pl.multiple_of((1 - core) * HALF, HALF), HALF)
    PO[...] = dot(attended, w_out[:, other], MAJOR).astype(BF16)
    in_o = send(PO, PI, o_s.at[0], o_r.at[0], sibling)
    own_part = dot(attended, w_out[:, mine], MAJOR)
    in_o.wait_recv()
    out[...] = (own_part + PI[...].astype(F32)).astype(BF16)
    for copy, here in backs:
        pl.when(here)(copy.wait_send)
    for copy in pending:
        copy.wait_send()


def shards(tiles, ln_gain, w_qkv, w_out, tile_source, tissue_count):
    dma = pltpu.SemaphoreType.DMA
    scratch = [
        pltpu.VMEM((D, 3 * ROWS), BF16),
        pltpu.VMEM((HALF, D), BF16),
        pltpu.VMEM((6, ROWS), F32),
        pltpu.VMEM((1, ROWS), jnp.int32),
        pltpu.SMEM((1,), jnp.int32),
        pltpu.VMEM((NX, 32, HALF), BF16),
        pltpu.VMEM((2 * NY, 16, HALF), BF16),
        pltpu.VMEM((NY, NZ, 16, HALF), BF16),
        pltpu.VMEM((NY, NZ, 16, HALF), BF16),
        pltpu.VMEM((SEG, 8, ROWS), F32),
        pltpu.VMEM((512, 3 * ROWS), BF16),
        pltpu.VMEM((512, 512), BF16),
        pltpu.VMEM((2, 160, 512), BF16),
        pltpu.VMEM((512, ROWS), BF16),
        pltpu.VMEM((512, ROWS), BF16),
        pltpu.VMEM((512, ROWS), BF16),
        pltpu.VMEM((NX, NY, 2, 72, ROWS), BF16),
        pltpu.VMEM((2, 2, 256, ROWS), BF16),
        pltpu.VMEM((SEG, 256, 256), BF16),
        pltpu.VMEM((SEG, 8, 256), F32),
        pltpu.VMEM((SEG, 8, 256), F32),
        pltpu.VMEM((SEG, ROWS, 256), F32),
        pltpu.VMEM((SEG, ROWS, ROWS), BF16),
        pltpu.VMEM((3, ROWS, ROWS), BF16),
        pltpu.VMEM((ROWS, HALF), BF16),
        pltpu.VMEM((ROWS, HALF), BF16),
        dma((5,)), dma((3,)),
    ]
    for size in (NX, NY * NZ, NY, SEG, NX * NY * 2, 4, SEG, 1):
        scratch += [dma((size,)), dma((size,))]
    anywhere = pl.BlockSpec(memory_space=pl.ANY)
    return pl.pallas_call(
        kernel,
        out_shape=jax.ShapeDtypeStruct((ROWS, HALF), BF16),
        in_specs=[anywhere] * 6,
        out_specs=pl.BlockSpec(memory_space=pltpu.VMEM),
        scratch_shapes=scratch,
        compiler_params=pltpu.CompilerParams(
            collective_id=0, has_side_effects=True, vmem_limit_bytes=48 << 20
        ),
    )(
        tiles.reshape(NX, 32, HALF),
        ln_gain.reshape(6, ROWS),
        jnp.transpose(w_qkv, (1, 0, 2)),
        w_out,
        tile_source.reshape(1, ROWS),
        tissue_count,
    )


def solution(mesh):
    return jax.shard_map(
        shards,
        mesh=mesh,
        in_specs=(
            P("seq", "head"),
            P(),
            P(None, None, "head"),
            P("head", None),
            P("seq"),
            P("seq"),
        ),
        out_specs=P("seq", "head"),
        check_vma=False,
    )
```

```python
import jax
import jax.numpy as jnp
from jax import lax
from jax.experimental import pallas as pl
from jax.experimental.pallas import tpu as pltpu
from jax.sharding import PartitionSpec as P

D = 768
HALF = 384
ROWS = 128
NX, NY, NZ = 4, 4, 8
SEG = 4
LONG = SEG * 8
NEG = -1e30
F32 = jnp.float32
BF16 = jnp.bfloat16
MESH = pl.DeviceIdType.MESH
PLAIN = (((1,), (0,)), ((), ()))
MINOR = (((1,), (1,)), ((), ()))
MAJOR = (((0,), (0,)), ((), ()))


def iota(shape, dim):
    return lax.broadcasted_iota(jnp.int32, shape, dim)


def dot(a, b, dims):
    return lax.dot_general(a, b, dims, preferred_element_type=F32)


def kernel(
    tiles, gain_in, w_qkv, w_out_in, src_in, cnt_in,
    out,
    w_v, w_out, gain, src, cnt, T, A, C, DD, E, SRC, R, PM, SEL,
    KS, VS, MKS, GF, HM, QA, M, L, O, AS, AT, PO, PI,
    w_sem, loc_sem,
    xs_s, xs_r, zs_s, zs_r, ps_s, ps_r, src_s, src_r,
    gf_s, gf_r, hm_s, hm_r, at_s, at_r, o_s, o_r,
):
    seq = lax.axis_index("seq")
    core = lax.axis_index("head")
    x, y, z = seq // (NY * NZ), (seq // NZ) % NY, seq % NZ
    zh, zj = z // SEG, z % SEG
    place = zj + zh * (SEG - 1 - 2 * zj)
    pair = (place + 1) // 2
    first_head = 6 * core + 2 * pair
    sibling = {"head": 1 - core}
    pending = []

    def at(px, py, pz):
        return {"seq": (px * NY + py) * NZ + pz}

    def remote(source, target, s_sem, r_sem, device):
        return pltpu.make_async_remote_copy(
            src_ref=source, dst_ref=target, send_sem=s_sem, recv_sem=r_sem,
            device_id=device, device_id_type=MESH,
        )

    def send(source, target, s_sem, r_sem, device):
        copy = remote(source, target, s_sem, r_sem, device)
        copy.start()
        pending.append(copy)
        return copy

    lanes = pl.ds(pl.multiple_of(pair * ROWS, ROWS), ROWS)
    weights = [
        pltpu.make_async_copy(w_qkv.at[t, :, lanes], w_v.at[:, t * ROWS : (t + 1) * ROWS], w_sem.at[t])
        for t in range(3)
    ]
    weights += [pltpu.make_async_copy(w_out_in, w_out, w_sem.at[3])]
    weights += [pltpu.make_async_copy(gain_in, gain, w_sem.at[4])]
    small = [
        pltpu.make_async_copy(src_in, src, loc_sem.at[1]),
        pltpu.make_async_copy(cnt_in, cnt, loc_sem.at[2]),
    ]
    own_t = pltpu.make_async_copy(tiles, T, loc_sem.at[0])
    barrier = pltpu.get_barrier_semaphore()
    peers = [at((x + k) % NX, y, z) for k in range(1, NX)] + [sibling]
    plane = [(o // NZ, o % NZ) for o in range(1, NY * NZ)]
    peers += [at(x, (y + dy) % NY, (z + dz) % NZ) for dy, dz in plane]
    for peer in peers:
        pl.semaphore_signal(barrier, inc=1, device_id=peer, device_id_type=MESH)
    for copy in small + [own_t] + weights:
        copy.start()
    for copy in small + [own_t]:
        copy.wait()
    own_count = cnt[0]
    rows8 = iota((8, ROWS), 0)
    tag = jnp.where(rows8 == 0, src[...] // ROWS, own_count)
    SRC[zj] = tag.astype(F32)
    pl.semaphore_wait(barrier, len(peers))

    in_x = [
        send(T.at[(x + k) % NX], A.at[k], xs_s.at[k], xs_r.at[k], at((x + k) % NX, y, z))
        for k in range(1, NX)
    ]
    in_src = [
        send(SRC.at[zj], SRC.at[zj], src_s.at[t], src_r.at[t], at(x, y, SEG * zh + (zj + t) % SEG))
        for t in range(1, SEG)
    ]
    A[0] = T[x]
    row, col = iota((ROWS, ROWS), 0), iota((ROWS, ROWS), 1)
    turn = (((row >> 2) & 3) * 32 + (row >> 4) * 4 + (row & 3) == col).astype(BF16)
    for copy in in_x:
        copy.wait_recv()
    turned = dot(turn, A[...].reshape(ROWS, HALF), PLAIN)
    C[...] = turned.astype(BF16).reshape(2 * NY, 16, HALF)

    in_z = [[] for _ in range(NY)]
    for dy, dz in plane:
        yt, zt = (y + dy) % NY, (z + dz) % NZ
        o = dy * NZ + dz
        in_z[dy].append(
            send(C.at[2 * yt + zt // SEG], DD.at[dy, dz], zs_s.at[o], zs_r.at[o], at(x, yt, zt))
        )
    DD[0, 0] = C[2 * y + zh]

    for copy in in_src:
        copy.wait_recv()
    lane512 = iota((1, 512), 1)
    from_x, from_y = (x + NX - ((lane512 >> 2) & 3)) & 3, (y + NY - (lane512 >> 7)) & 3
    from_z = (z + NZ - ((lane512 >> 4) & 7)) & 7
    code = (((from_x * NY + from_y) * NZ + from_z) * SEG + (lane512 & 3)).astype(F32)
    place_iota = iota((ROWS, ROWS), 0).astype(F32)
    for b in range(SEG):
        block = SRC[b]
        wanted = jnp.transpose(block)[:, 0:1] * SEG + b
        PM[b * ROWS : (b + 1) * ROWS] = (wanted == code).astype(BF16)
        alive = place_iota < block[1:2]
        MKS[b * ROWS : (b + 1) * ROWS] = jnp.where(alive, 0.0, NEG).astype(BF16)
        AS[b] = (iota((ROWS, ROWS), 1).astype(F32) < block[1:2]).astype(BF16)
        GF[0, 0, 0, 64 + b : 65 + b] = block[1:2].astype(BF16)
        QA[b, 0:ROWS, ROWS:] = (col == 0).astype(BF16)
        QA[b, ROWS:, ROWS:] = (col == 1).astype(BF16)
        M[b] = jnp.full((8, 256), NEG, F32)
        L[b] = jnp.zeros((8, 256), F32)
        O[b] = jnp.zeros((ROWS, 256), F32)
    GF[0, 0, 0, 68:72] = jnp.zeros((4, ROWS), BF16)
    out_row, from_row = iota((160, 512), 0), iota((160, 512), 1)
    for h in range(2):
        head = first_head + h
        mid = (out_row >> 5) * ROWS + (out_row & 31) * 4 + head % 4
        far_row = out_row - ROWS
        far = (far_row >> 3) * ROWS + (far_row & 7) * 16 + head
        SEL[h] = (jnp.where(out_row < ROWS, mid, far) == from_row).astype(BF16)
    for copy in weights:
        copy.wait()

    gain_mine = jnp.concatenate([gain[pl.ds(3 * core + i, 1)] for i in range(3)], axis=1)
    gain_other = jnp.concatenate([gain[pl.ds(3 - 3 * core + i, 1)] for i in range(3)], axis=1)
    w_mine = w_v[pl.ds(pl.multiple_of(core * HALF, HALF), HALF)]
    w_other = w_v[pl.ds(pl.multiple_of((1 - core) * HALF, HALF), HALF)]
    in_p = []

    def project(c):
        a = DD[c].reshape(ROWS, HALF).astype(F32)
        b = E[c].reshape(ROWS, HALF).astype(F32)
        mean = (jnp.sum(a, 1, keepdims=True) + jnp.sum(b, 1, keepdims=True)) / D
        a, b = a - mean, b - mean
        var = (jnp.sum(a * a, 1, keepdims=True) + jnp.sum(b * b, 1, keepdims=True)) / D
        scale = lax.rsqrt(var + 1e-05)
        a = (a * scale * gain_mine).astype(BF16)
        b = (b * scale * gain_other).astype(BF16)
        R[c * ROWS : (c + 1) * ROWS] = (dot(a, w_mine, PLAIN) + dot(b, w_other, PLAIN)).astype(BF16)

    for c in range(NY):
        for copy in in_z[c]:
            copy.wait_recv()
        in_p.append(send(DD.at[c], E.at[c], ps_s.at[c], ps_r.at[c], sibling))
        if c:
            in_p[c - 1].wait_recv()
            project(c - 1)
    in_p[NY - 1].wait_recv()
    project(NY - 1)

    qkv = dot(PM[...], R[...], PLAIN)
    kv = qkv[:, ROWS:].astype(BF16)
    low = (iota((1, 2 * ROWS), 1) & 127) < 64
    picked = jnp.where(low, dot(SEL[0], kv, PLAIN), dot(SEL[1], kv, PLAIN)).astype(BF16)
    HM[0, 0, 0:ROWS] = picked[0:ROWS, 0:ROWS]
    HM[0, 0, ROWS:] = picked[0:ROWS, ROWS:]
    GF[0, 0, 0, 0:LONG] = picked[ROWS:, 0:ROWS]
    GF[0, 0, 0, LONG : 2 * LONG] = picked[ROWS:, ROWS:]

    def to_xy(f, o):
        dx, dy = o // NY, o % NY
        return send(
            GF.at[0, 0, f], GF.at[dx, dy, f], gf_s.at[2 * o + f], gf_r.at[2 * o + f],
            at((x + dx) % NX, (y + dy) % NY, z),
        )

    def middle(yy, f, source, device):
        o = 2 * yy + f
        return send(source, HM.at[yy, f], hm_s.at[o], hm_r.at[o], device)

    mirror, partner = at(x, y, NZ - 1 - z), at(x, y + 1 - 2 * (y % 2), z)
    order = (10, 11, 9, 14, 6, 2, 8, 3, 1, 12, 4, 7, 13, 15, 5)
    in_far = send(GF.at[0, 0, 0], GF.at[0, 0, 1], gf_s.at[1], gf_r.at[1], mirror)
    in_m01 = middle(0, 1, HM.at[0, 0], mirror)
    in_near = {o: to_xy(0, o) for o in order}
    in_m10 = middle(1, 0, HM.at[0, 0], partner)
    KS[...] = kv[:, 0:ROWS]
    VS[...] = kv[:, ROWS:]
    q32 = qkv[:, 0:ROWS].astype(BF16).astype(F32) * 0.125
    for b in range(SEG):
        q_b = q32[b * ROWS : (b + 1) * ROWS]
        QA[b, 0:ROWS, 0:ROWS] = jnp.where(col < 64, q_b, 0.0).astype(BF16)
        QA[b, ROWS:, 0:ROWS] = jnp.where(col < 64, 0.0, q_b).astype(BF16)

    def absorb(keys, values, masks, finish=None):
        keys = jnp.concatenate([keys, masks], axis=1)
        for b in range(SEG):
            scores = dot(keys, QA[b], MINOR)
            old = M[b][0:1]
            new = jnp.maximum(old, jnp.max(scores, axis=0, keepdims=True))
            weight = jnp.exp(scores - new)
            rescale = jnp.exp(old - new)
            total = L[b][0:1] * rescale + jnp.sum(weight, axis=0, keepdims=True)
            O[b] = O[b] * rescale + dot(values, weight.astype(BF16), MAJOR)
            M[b] = jnp.broadcast_to(new, (8, 256))
            L[b] = jnp.broadcast_to(total, (8, 256))
            if finish is not None:
                finish(b)

    def mask(n, counts, segment_rows, stride):
        r, c = iota((n, counts.shape[0]), 0), iota((n, counts.shape[0]), 1)
        per_block = segment_rows // SEG
        owner = ((r // segment_rows) * 8 + (r % segment_rows) // per_block == c).astype(BF16)
        position = (iota((n, ROWS), 0) % per_block) * stride
        position = position + (first_head + jnp.minimum(iota((n, ROWS), 1), 1)) % stride
        alive = position.astype(F32) < dot(owner, counts, PLAIN)
        return jnp.where(alive, 0.0, NEG).astype(BF16)

    in_far.wait_recv()
    in_other = {o: to_xy(1, o) for o in order}
    absorb(KS[...], VS[...], MKS[...])
    in_m01.wait_recv()
    in_m11 = middle(1, 1, HM.at[0, 1], partner)

    def whole(dx, f, finish=None):
        tags = GF[dx : dx + 2, :, f, 64:72].astype(F32).reshape(64, ROWS).astype(BF16)
        absorb(
            GF[dx : dx + 2, :, f, 0:LONG].reshape(256, ROWS),
            GF[dx : dx + 2, :, f, LONG : 2 * LONG].reshape(256, ROWS),
            mask(256, tags, LONG, 16),
            finish,
        )

    for dx in (0, 2):
        for o in order:
            if o // NY in (dx, dx + 1):
                in_near[o].wait_recv()
        whole(dx, 0)
    in_other[1].wait_recv()
    in_other[3].wait_recv()
    in_m10.wait_recv()
    in_m11.wait_recv()
    tags = [GF[0, 0, 0, 64:72], GF[0, 0, 1, 64:72]]
    slot = NY - 1 - 2 * (y % 2)
    tags += [GF[0, slot, 0, 64:72], GF[0, slot, 1, 64:72]]
    tags = jnp.concatenate([part.astype(F32) for part in tags], axis=0).astype(BF16)
    absorb(
        HM[:, :, 0:ROWS].reshape(512, ROWS),
        HM[:, :, ROWS:].reshape(512, ROWS),
        mask(512, tags, ROWS, 4),
    )
    backs = []

    def give_back(b):
        halves = []
        for h in range(2):
            cols = slice(h * ROWS, (h + 1) * ROWS)
            halves.append(O[b][h * 64 : (h + 1) * 64, cols] / L[b][0:1, cols])
        AS[b] = (jnp.concatenate(halves, axis=0) * AS[b].astype(F32)).astype(BF16)
        target = b + zh * (SEG - 1 - 2 * b)
        here = (place == 0) | (place == 3)
        here = here | ((place == 1) & (target == 0)) | ((place == 2) & (target == 3))
        here = here & (place != target)
        copy = remote(AS.at[b], AT.at[pair], at_s.at[b], at_r.at[pair], at(x, y, SEG * zh + b))
        backs.append((copy, here))
        pl.when(here)(copy.start)

    for dx in (0, 2):
        for o in order:
            if o // NY in (dx, dx + 1) and o not in (1, 3):
                in_other[o].wait_recv()
        whole(dx, 1, give_back if dx else None)
    AT[pair] = AS[zj]
    for g in range(3):
        arrival = remote(AS.at[0], AT.at[g], at_s.at[0], at_r.at[g], sibling)
        pl.when(pair != g)(arrival.wait_recv)
    attended = AT[...].reshape(HALF, ROWS)
    mine = pl.ds(pl.multiple_of(core * HALF, HALF), HALF)
    other = pl.ds(pl.multiple_of((1 - core) * HALF, HALF), HALF)
    PO[...] = dot(attended, w_out[:, other], MAJOR).astype(BF16)
    in_o = send(PO, PI, o_s.at[0], o_r.at[0], sibling)
    own_part = dot(attended, w_out[:, mine], MAJOR)
    in_o.wait_recv()
    out[...] = (own_part + PI[...].astype(F32)).astype(BF16)
    for copy, here in backs:
        pl.when(here)(copy.wait_send)
    for copy in pending:
        copy.wait_send()


def shards(tiles, ln_gain, w_qkv, w_out, tile_source, tissue_count):
    dma = pltpu.SemaphoreType.DMA
    scratch = [
        pltpu.VMEM((D, 3 * ROWS), BF16),
        pltpu.VMEM((HALF, D), BF16),
        pltpu.VMEM((6, ROWS), F32),
        pltpu.VMEM((1, ROWS), jnp.int32),
        pltpu.SMEM((1,), jnp.int32),
        pltpu.VMEM((NX, 32, HALF), BF16),
        pltpu.VMEM((NX, 32, HALF), BF16),
        pltpu.VMEM((2 * NY, 16, HALF), BF16),
        pltpu.VMEM((NY, NZ, 16, HALF), BF16),
        pltpu.VMEM((NY, NZ, 16, HALF), BF16),
        pltpu.VMEM((SEG, 8, ROWS), F32),
        pltpu.VMEM((512, 3 * ROWS), BF16),
        pltpu.VMEM((512, 512), BF16),
        pltpu.VMEM((2, 160, 512), BF16),
        pltpu.VMEM((512, ROWS), BF16),
        pltpu.VMEM((512, ROWS), BF16),
        pltpu.VMEM((512, ROWS), BF16),
        pltpu.VMEM((NX, NY, 2, 72, ROWS), BF16),
        pltpu.VMEM((2, 2, 256, ROWS), BF16),
        pltpu.VMEM((SEG, 256, 256), BF16),
        pltpu.VMEM((SEG, 8, 256), F32),
        pltpu.VMEM((SEG, 8, 256), F32),
        pltpu.VMEM((SEG, ROWS, 256), F32),
        pltpu.VMEM((SEG, ROWS, ROWS), BF16),
        pltpu.VMEM((3, ROWS, ROWS), BF16),
        pltpu.VMEM((ROWS, HALF), BF16),
        pltpu.VMEM((ROWS, HALF), BF16),
        dma((5,)), dma((3,)),
    ]
    for size in (NX, NY * NZ, NY, SEG, NX * NY * 2, 4, SEG, 1):
        scratch += [dma((size,)), dma((size,))]
    anywhere = pl.BlockSpec(memory_space=pltpu.HBM)
    return pl.pallas_call(
        kernel,
        out_shape=jax.ShapeDtypeStruct((ROWS, HALF), BF16),
        in_specs=[anywhere] * 6,
        out_specs=pl.BlockSpec(memory_space=pltpu.VMEM),
        scratch_shapes=scratch,
        compiler_params=pltpu.CompilerParams(
            collective_id=0, has_side_effects=True, vmem_limit_bytes=64 << 20
        ),
    )(
        tiles.reshape(NX, 32, HALF),
        ln_gain.reshape(6, ROWS),
        jnp.transpose(w_qkv, (1, 0, 2)),
        w_out,
        tile_source.reshape(1, ROWS),
        tissue_count,
    )


def solution(mesh):
    return jax.shard_map(
        shards,
        mesh=mesh,
        in_specs=(
            P("seq", "head"),
            P(),
            P(None, None, "head"),
            P("head", None),
            P("seq"),
            P("seq"),
        ),
        out_specs=P("seq", "head"),
        check_vma=False,
    )
```

```python
import jax
import jax.numpy as jnp
from jax import lax
from jax.experimental import pallas as pl
from jax.experimental.pallas import tpu as pltpu
from jax.sharding import PartitionSpec as P

D = 768
HALF = 384
ROWS = 128
NX, NY, NZ = 4, 4, 8
SEG = 4
LONG = SEG * 8
NEG = -1e30
F32 = jnp.float32
BF16 = jnp.bfloat16
MESH = pl.DeviceIdType.MESH
PLAIN = (((1,), (0,)), ((), ()))
MINOR = (((1,), (1,)), ((), ()))
MAJOR = (((0,), (0,)), ((), ()))


def iota(shape, dim):
    return lax.broadcasted_iota(jnp.int32, shape, dim)


def dot(a, b, dims):
    return lax.dot_general(a, b, dims, preferred_element_type=F32)


def kernel(
    tiles, gain_in, w_qkv, w_out_in, src_in, cnt_in,
    own_part, other_part,
    w_v, w_out, gain, src, cnt, T, A, C, DD, E, SRC, R, PM, SEL,
    KS, VS, MKS, GF, HM, QA, M, L, O, AS, AT, PO, OWN,
    w_sem, loc_sem, ready,
    xs_s, xs_r, zs_s, zs_r, ps_s, ps_r, src_s, src_r,
    gf_s, gf_r, hm_s, hm_r, at_s, at_r, o_s, o_r,
):
    seq = lax.axis_index("seq")
    core = lax.axis_index("head")
    x, y, z = seq // (NY * NZ), (seq // NZ) % NY, seq % NZ
    zh, zj = z // SEG, z % SEG
    place = zj + zh * (SEG - 1 - 2 * zj)
    pair = place % 3
    first_head = 6 * core + 2 * pair
    sibling = {"head": 1 - core}
    pending = []

    def at(px, py, pz):
        return {"seq": (px * NY + py) * NZ + pz}

    def remote(source, target, s_sem, r_sem, device):
        return pltpu.make_async_remote_copy(
            src_ref=source, dst_ref=target, send_sem=s_sem, recv_sem=r_sem,
            device_id=device, device_id_type=MESH,
        )

    def send(source, target, s_sem, r_sem, device):
        copy = remote(source, target, s_sem, r_sem, device)
        copy.start()
        pending.append(copy)
        return copy

    lanes = pl.ds(pl.multiple_of(pair * ROWS, ROWS), ROWS)
    weights = [
        pltpu.make_async_copy(w_qkv.at[t, :, lanes], w_v.at[:, t * ROWS : (t + 1) * ROWS], w_sem.at[t])
        for t in range(3)
    ]
    weights += [pltpu.make_async_copy(w_out_in, w_out, w_sem.at[3])]
    weights += [pltpu.make_async_copy(gain_in, gain, w_sem.at[4])]
    small = [
        pltpu.make_async_copy(src_in, src, loc_sem.at[1]),
        pltpu.make_async_copy(cnt_in, cnt, loc_sem.at[2]),
    ]
    own_t = pltpu.make_async_copy(tiles, T, loc_sem.at[0])
    barrier = pltpu.get_barrier_semaphore()
    peers = [at((x + k) % NX, y, z) for k in range(1, NX)] + [sibling]
    plane = [(o // NZ, o % NZ) for o in range(1, NY * NZ)]
    y_peers = [at(x, (y + k) % NY, z) for k in range(1, NY)]
    peers += y_peers + [at(x, y, (z + k) % NZ) for k in range(1, NZ)]
    for peer in peers:
        pl.semaphore_signal(barrier, inc=1, device_id=peer, device_id_type=MESH)
    for copy in small + [own_t] + weights:
        copy.start()
    for copy in small + [own_t]:
        copy.wait()
    own_count = cnt[0]
    rows8 = iota((8, ROWS), 0)
    tag = jnp.where(rows8 == 0, src[...] // ROWS, own_count)
    SRC[zj] = tag.astype(F32)
    pl.semaphore_wait(barrier, len(peers))
    for peer in y_peers:
        pl.semaphore_signal(ready, inc=1, device_id=peer, device_id_type=MESH)

    in_x = [
        send(T.at[(x + k) % NX], A.at[k], xs_s.at[k], xs_r.at[k], at((x + k) % NX, y, z))
        for k in range(1, NX)
    ]
    in_src = [
        send(SRC.at[zj], SRC.at[zj], src_s.at[t], src_r.at[t], at(x, y, SEG * zh + (zj + t) % SEG))
        for t in range(1, SEG)
    ]
    A[0] = T[x]
    row, col = iota((ROWS, ROWS), 0), iota((ROWS, ROWS), 1)
    turn = (((row >> 2) & 3) * 32 + (row >> 4) * 4 + (row & 3) == col).astype(BF16)
    for copy in in_x:
        copy.wait_recv()
    pl.semaphore_wait(ready, len(y_peers))
    turned = dot(turn, A[...].reshape(ROWS, HALF), PLAIN)
    C[...] = turned.astype(BF16).reshape(2 * NY, 16, HALF)

    in_z = [[] for _ in range(NY)]
    for dy, dz in plane:
        yt, zt = (y + dy) % NY, (z + dz) % NZ
        o = dy * NZ + dz
        in_z[dy].append(
            send(C.at[2 * yt + zt // SEG], DD.at[dy, dz], zs_s.at[o], zs_r.at[o], at(x, yt, zt))
        )
    DD[0, 0] = C[2 * y + zh]

    for copy in in_src:
        copy.wait_recv()
    lane512 = iota((1, 512), 1)
    from_x, from_y = (x + NX - ((lane512 >> 2) & 3)) & 3, (y + NY - (lane512 >> 7)) & 3
    from_z = (z + NZ - ((lane512 >> 4) & 7)) & 7
    code = (((from_x * NY + from_y) * NZ + from_z) * SEG + (lane512 & 3)).astype(F32)
    place_iota = iota((ROWS, ROWS), 0).astype(F32)
    for b in range(SEG):
        block = SRC[b]
        wanted = jnp.transpose(block)[:, 0:1] * SEG + b
        PM[b * ROWS : (b + 1) * ROWS] = (wanted == code).astype(BF16)
        alive = place_iota < block[1:2]
        MKS[b * ROWS : (b + 1) * ROWS] = jnp.where(alive, 0.0, NEG).astype(BF16)
        AS[b] = (iota((ROWS, ROWS), 1).astype(F32) < block[1:2]).astype(BF16)
        GF[0, 0, 0, 64 + b : 65 + b] = block[1:2].astype(BF16)
        QA[b, 0:ROWS, ROWS:] = (col == 0).astype(BF16)
        QA[b, ROWS:, ROWS:] = (col == 1).astype(BF16)
        M[b] = jnp.full((8, 256), NEG, F32)
        L[b] = jnp.zeros((8, 256), F32)
        O[b] = jnp.zeros((ROWS, 256), F32)
    GF[0, 0, 0, 68:72] = jnp.zeros((4, ROWS), BF16)
    out_row, from_row = iota((160, 512), 0), iota((160, 512), 1)
    for h in range(2):
        head = first_head + h
        mid = (out_row >> 5) * ROWS + (out_row & 31) * 4 + head % 4
        far_row = out_row - ROWS
        far = (far_row >> 3) * ROWS + (far_row & 7) * 16 + head
        SEL[h] = (jnp.where(out_row < ROWS, mid, far) == from_row).astype(BF16)
    for copy in weights:
        copy.wait()

    gain_mine = jnp.concatenate([gain[pl.ds(3 * core + i, 1)] for i in range(3)], axis=1)
    gain_other = jnp.concatenate([gain[pl.ds(3 - 3 * core + i, 1)] for i in range(3)], axis=1)
    w_mine = w_v[pl.ds(pl.multiple_of(core * HALF, HALF), HALF)]
    w_other = w_v[pl.ds(pl.multiple_of((1 - core) * HALF, HALF), HALF)]
    in_p = []

    def project(c):
        a = DD[c].reshape(ROWS, HALF).astype(F32)
        b = E[c].reshape(ROWS, HALF).astype(F32)
        mean = (jnp.sum(a, 1, keepdims=True) + jnp.sum(b, 1, keepdims=True)) / D
        a, b = a - mean, b - mean
        var = (jnp.sum(a * a, 1, keepdims=True) + jnp.sum(b * b, 1, keepdims=True)) / D
        scale = lax.rsqrt(var + 1e-05)
        a = (a * scale * gain_mine).astype(BF16)
        b = (b * scale * gain_other).astype(BF16)
        R[c * ROWS : (c + 1) * ROWS] = (dot(a, w_mine, PLAIN) + dot(b, w_other, PLAIN)).astype(BF16)

    for c in range(NY):
        for copy in in_z[c]:
            copy.wait_recv()
        in_p.append(send(DD.at[c], E.at[c], ps_s.at[c], ps_r.at[c], sibling))
        if c:
            in_p[c - 1].wait_recv()
            project(c - 1)
    in_p[NY - 1].wait_recv()
    project(NY - 1)

    qkv = dot(PM[...], R[...], PLAIN)
    kv = qkv[:, ROWS:].astype(BF16)
    low = (iota((1, 2 * ROWS), 1) & 127) < 64
    picked = jnp.where(low, dot(SEL[0], kv, PLAIN), dot(SEL[1], kv, PLAIN)).astype(BF16)
    HM[0, 0, 0:ROWS] = picked[0:ROWS, 0:ROWS]
    HM[0, 0, ROWS:] = picked[0:ROWS, ROWS:]
    GF[0, 0, 0, 0:LONG] = picked[ROWS:, 0:ROWS]
    GF[0, 0, 0, LONG : 2 * LONG] = picked[ROWS:, ROWS:]

    def to_xy(f, o):
        dx, dy = o // NY, o % NY
        return send(
            GF.at[0, 0, f], GF.at[dx, dy, f], gf_s.at[2 * o + f], gf_r.at[2 * o + f],
            at((x + dx) % NX, (y + dy) % NY, z),
        )

    def middle(yy, f, source, device):
        o = 2 * yy + f
        return send(source, HM.at[yy, f], hm_s.at[o], hm_r.at[o], device)

    mirror, partner = at(x, y, NZ - 1 - z), at(x, y + 1 - 2 * (y % 2), z)
    order = (10, 11, 9, 14, 6, 2, 8, 3, 1, 12, 4, 7, 13, 15, 5)
    in_far = send(GF.at[0, 0, 0], GF.at[0, 0, 1], gf_s.at[1], gf_r.at[1], mirror)
    in_m01 = middle(0, 1, HM.at[0, 0], mirror)
    in_near = {o: to_xy(0, o) for o in order}
    in_m10 = middle(1, 0, HM.at[0, 0], partner)
    KS[...] = kv[:, 0:ROWS]
    VS[...] = kv[:, ROWS:]
    q32 = qkv[:, 0:ROWS].astype(BF16).astype(F32) * 0.125
    for b in range(SEG):
        q_b = q32[b * ROWS : (b + 1) * ROWS]
        QA[b, 0:ROWS, 0:ROWS] = jnp.where(col < 64, q_b, 0.0).astype(BF16)
        QA[b, ROWS:, 0:ROWS] = jnp.where(col < 64, 0.0, q_b).astype(BF16)

    def absorb(keys, values, masks, finish=None):
        keys = jnp.concatenate([keys, masks], axis=1)
        turned_values = jnp.transpose(values)
        blocks = range(SEG)
        scores = [dot(keys, QA[b], MINOR) for b in blocks]
        old = [M[b][0:1] for b in blocks]
        new = [jnp.maximum(old[b], jnp.max(scores[b], axis=0, keepdims=True)) for b in blocks]
        weight = [jnp.exp(scores[b] - new[b]) for b in blocks]
        rescale = [jnp.exp(old[b] - new[b]) for b in blocks]
        mixed = [dot(turned_values, weight[b].astype(BF16), PLAIN) for b in blocks]
        for b in blocks:
            total = L[b][0:1] * rescale[b] + jnp.sum(weight[b], axis=0, keepdims=True)
            O[b] = O[b] * rescale[b] + mixed[b]
            M[b] = jnp.broadcast_to(new[b], (8, 256))
            L[b] = jnp.broadcast_to(total, (8, 256))
            if finish is not None:
                finish(b)

    def mask(n, counts, segment_rows, stride):
        r, c = iota((n, counts.shape[0]), 0), iota((n, counts.shape[0]), 1)
        per_block = segment_rows // SEG
        owner = ((r // segment_rows) * 8 + (r % segment_rows) // per_block == c).astype(BF16)
        position = (iota((n, ROWS), 0) % per_block) * stride
        position = position + (first_head + jnp.minimum(iota((n, ROWS), 1), 1)) % stride
        alive = position.astype(F32) < dot(owner, counts, PLAIN)
        return jnp.where(alive, 0.0, NEG).astype(BF16)

    absorb(KS[...], VS[...], MKS[...])
    in_far.wait_recv()
    in_other = {o: to_xy(1, o) for o in order}
    in_m01.wait_recv()
    in_m11 = middle(1, 1, HM.at[0, 1], partner)

    def whole(dx, f, finish=None):
        tags = GF[dx : dx + 2, :, f, 64:72].astype(F32).reshape(64, ROWS).astype(BF16)
        absorb(
            GF[dx : dx + 2, :, f, 0:LONG].reshape(256, ROWS),
            GF[dx : dx + 2, :, f, LONG : 2 * LONG].reshape(256, ROWS),
            mask(256, tags, LONG, 16),
            finish,
        )

    for dx in (0, 2):
        for o in order:
            if o // NY in (dx, dx + 1):
                in_near[o].wait_recv()
        whole(dx, 0)
    in_other[1].wait_recv()
    in_other[3].wait_recv()
    in_m10.wait_recv()
    in_m11.wait_recv()
    tags = [GF[0, 0, 0, 64:72], GF[0, 0, 1, 64:72]]
    slot = NY - 1 - 2 * (y % 2)
    tags += [GF[0, slot, 0, 64:72], GF[0, slot, 1, 64:72]]
    tags = jnp.concatenate([part.astype(F32) for part in tags], axis=0).astype(BF16)
    absorb(
        HM[:, :, 0:ROWS].reshape(512, ROWS),
        HM[:, :, ROWS:].reshape(512, ROWS),
        mask(512, tags, ROWS, 4),
    )
    backs = []

    def give_back(b):
        halves = []
        for h in range(2):
            cols = slice(h * ROWS, (h + 1) * ROWS)
            halves.append(O[b][h * 64 : (h + 1) * 64, cols] / L[b][0:1, cols])
        AS[b] = (jnp.concatenate(halves, axis=0) * AS[b].astype(F32)).astype(BF16)
        target = b + zh * (SEG - 1 - 2 * b)
        here = (place == 1) | (place == 2)
        here = here | ((place == 0) & (target == 1)) | ((place == 3) & (target == 2))
        here = here & (place != target)
        copy = remote(AS.at[b], AT.at[pair], at_s.at[b], at_r.at[pair], at(x, y, SEG * zh + b))
        backs.append((copy, here))
        pl.when(here)(copy.start)

    for dx in (0, 2):
        for o in order:
            if o // NY in (dx, dx + 1) and o not in (1, 3):
                in_other[o].wait_recv()
        whole(dx, 1, give_back if dx else None)
    AT[pair] = AS[zj]
    for g in range(3):
        arrival = remote(AS.at[0], AT.at[g], at_s.at[0], at_r.at[g], sibling)
        pl.when(pair != g)(arrival.wait_recv)
    attended = AT[...].reshape(HALF, ROWS)
    mine = pl.ds(pl.multiple_of(core * HALF, HALF), HALF)
    other = pl.ds(pl.multiple_of((1 - core) * HALF, HALF), HALF)
    PO[...] = dot(attended, w_out[:, other], MAJOR).astype(BF16)
    in_o = send(PO, other_part, o_s.at[0], o_r.at[0], sibling)
    OWN[...] = dot(attended, w_out[:, mine], MAJOR)
    hand_out = pltpu.make_async_copy(OWN, own_part, loc_sem.at[0])
    hand_out.start()
    hand_out.wait()
    in_o.wait_recv()
    for copy, here in backs:
        pl.when(here)(copy.wait_send)
    for copy in pending:
        copy.wait_send()


def shards(tiles, ln_gain, w_qkv, w_out, tile_source, tissue_count):
    dma = pltpu.SemaphoreType.DMA
    scratch = [
        pltpu.VMEM((D, 3 * ROWS), BF16),
        pltpu.VMEM((HALF, D), BF16),
        pltpu.VMEM((6, ROWS), F32),
        pltpu.VMEM((1, ROWS), jnp.int32),
        pltpu.SMEM((1,), jnp.int32),
        pltpu.VMEM((NX, 32, HALF), BF16),
        pltpu.VMEM((NX, 32, HALF), BF16),
        pltpu.VMEM((2 * NY, 16, HALF), BF16),
        pltpu.VMEM((NY, NZ, 16, HALF), BF16),
        pltpu.VMEM((NY, NZ, 16, HALF), BF16),
        pltpu.VMEM((SEG, 8, ROWS), F32),
        pltpu.VMEM((512, 3 * ROWS), BF16),
        pltpu.VMEM((512, 512), BF16),
        pltpu.VMEM((2, 160, 512), BF16),
        pltpu.VMEM((512, ROWS), BF16),
        pltpu.VMEM((512, ROWS), BF16),
        pltpu.VMEM((512, ROWS), BF16),
        pltpu.VMEM((NX, NY, 2, 72, ROWS), BF16),
        pltpu.VMEM((2, 2, 256, ROWS), BF16),
        pltpu.VMEM((SEG, 256, 256), BF16),
        pltpu.VMEM((SEG, 8, 256), F32),
        pltpu.VMEM((SEG, 8, 256), F32),
        pltpu.VMEM((SEG, ROWS, 256), F32),
        pltpu.VMEM((SEG, ROWS, ROWS), BF16),
        pltpu.VMEM((3, ROWS, ROWS), BF16),
        pltpu.VMEM((ROWS, HALF), BF16),
        pltpu.VMEM((ROWS, HALF), F32),
        dma((5,)), dma((3,)), pltpu.SemaphoreType.REGULAR,
    ]
    for size in (NX, NY * NZ, NY, SEG, NX * NY * 2, 4, SEG, 1):
        scratch += [dma((size,)), dma((size,))]
    anywhere = pl.BlockSpec(memory_space=pltpu.HBM)
    own_part, other_part = pl.pallas_call(
        kernel,
        out_shape=(
            jax.ShapeDtypeStruct((ROWS, HALF), F32),
            jax.ShapeDtypeStruct((ROWS, HALF), BF16),
        ),
        in_specs=[anywhere] * 6,
        out_specs=(anywhere, anywhere),
        scratch_shapes=scratch,
        compiler_params=pltpu.CompilerParams(
            collective_id=0, has_side_effects=True, vmem_limit_bytes=64 << 20
        ),
    )(
        tiles.reshape(NX, 32, HALF),
        ln_gain.reshape(6, ROWS),
        jnp.transpose(w_qkv, (1, 0, 2)),
        w_out,
        tile_source.reshape(1, ROWS),
        tissue_count,
    )
    return (own_part + other_part.astype(F32)).astype(BF16)


def solution(mesh):
    return jax.shard_map(
        shards,
        mesh=mesh,
        in_specs=(
            P("seq", "head"),
            P(),
            P(None, None, "head"),
            P("head", None),
            P("seq"),
            P("seq"),
        ),
        out_specs=P("seq", "head"),
        check_vma=False,
    )
```

```python
import jax
import jax.numpy as jnp
from jax import lax
from jax.experimental import pallas as pl
from jax.experimental.pallas import tpu as pltpu
from jax.sharding import PartitionSpec as P

D = 768
HALF = 384
ROWS = 128
NX, NY, NZ = 4, 4, 8
SEG = 4
LONG = SEG * 8
NEG = -1e30
F32 = jnp.float32
BF16 = jnp.bfloat16
MESH = pl.DeviceIdType.MESH
PLAIN = (((1,), (0,)), ((), ()))
MINOR = (((1,), (1,)), ((), ()))
MAJOR = (((0,), (0,)), ((), ()))


def iota(shape, dim):
    return lax.broadcasted_iota(jnp.int32, shape, dim)


def dot(a, b, dims):
    return lax.dot_general(a, b, dims, preferred_element_type=F32)


def kernel(
    tiles, gain_in, w_qkv, w_out_in, src_in, cnt_in,
    own_part, other_part,
    w_v, w_out, gain, src, cnt, T, A, C, DD, E, SRC, R, PM, SEL,
    KS, VS, MKS, MKM, MKL, CX, CY, CZ, GF, HM, QA, M, L, O, AS, AT, PO, OWN,
    w_sem, loc_sem, ready,
    xs_s, xs_r, zs_s, zs_r, ps_s, ps_r, src_s, src_r,
    gf_s, gf_r, hm_s, hm_r, at_s, at_r, o_s, o_r,
    cx_s, cx_r, cy_s, cy_r, cz_s, cz_r,
):
    seq = lax.axis_index("seq")
    core = lax.axis_index("head")
    x, y, z = seq // (NY * NZ), (seq // NZ) % NY, seq % NZ
    zh, zj = z // SEG, z % SEG
    place = zj + zh * (SEG - 1 - 2 * zj)
    pair = place % 3
    first_head = 6 * core + 2 * pair
    sibling = {"head": 1 - core}
    pending = []

    def at(px, py, pz):
        return {"seq": (px * NY + py) * NZ + pz}

    def remote(source, target, s_sem, r_sem, device):
        return pltpu.make_async_remote_copy(
            src_ref=source, dst_ref=target, send_sem=s_sem, recv_sem=r_sem,
            device_id=device, device_id_type=MESH,
        )

    def send(source, target, s_sem, r_sem, device):
        copy = remote(source, target, s_sem, r_sem, device)
        copy.start()
        pending.append(copy)
        return copy

    lanes = pl.ds(pl.multiple_of(pair * ROWS, ROWS), ROWS)
    weights = [
        pltpu.make_async_copy(w_qkv.at[t, :, lanes], w_v.at[:, t * ROWS : (t + 1) * ROWS], w_sem.at[t])
        for t in range(3)
    ]
    weights += [pltpu.make_async_copy(w_out_in, w_out, w_sem.at[3])]
    weights += [pltpu.make_async_copy(gain_in, gain, w_sem.at[4])]
    small = [
        pltpu.make_async_copy(src_in, src, loc_sem.at[1]),
        pltpu.make_async_copy(cnt_in, cnt, loc_sem.at[2]),
    ]
    own_t = pltpu.make_async_copy(tiles, T, loc_sem.at[0])
    barrier = pltpu.get_barrier_semaphore()
    peers = [at((x + k) % NX, y, z) for k in range(1, NX)] + [sibling]
    plane = [(o // NZ, o % NZ) for o in range(1, NY * NZ)]
    y_peers = [at(x, (y + k) % NY, z) for k in range(1, NY)]
    peers += y_peers + [at(x, y, (z + k) % NZ) for k in range(1, NZ)]
    for peer in peers:
        pl.semaphore_signal(barrier, inc=1, device_id=peer, device_id_type=MESH)
    for copy in small + [own_t] + weights:
        copy.start()
    for copy in small + [own_t]:
        copy.wait()
    own_count = cnt[0]
    rows8 = iota((8, ROWS), 0)
    tag = jnp.where(rows8 == 0, src[...] // ROWS, own_count)
    SRC[zj] = tag.astype(F32)
    CX[0] = jnp.where(iota((8, ROWS), 1) == seq, own_count, 0).astype(F32)
    pl.semaphore_wait(barrier, len(peers))
    for peer in y_peers:
        pl.semaphore_signal(ready, inc=1, device_id=peer, device_id_type=MESH)

    in_x = [
        send(T.at[(x + k) % NX], A.at[k], xs_s.at[k], xs_r.at[k], at((x + k) % NX, y, z))
        for k in range(1, NX)
    ]
    in_cx = [
        send(CX.at[0], CX.at[k], cx_s.at[k], cx_r.at[k], at((x + k) % NX, y, z))
        for k in range(1, NX)
    ]
    in_src = [
        send(SRC.at[zj], SRC.at[zj], src_s.at[t], src_r.at[t], at(x, y, SEG * zh + (zj + t) % SEG))
        for t in range(1, SEG)
    ]
    A[0] = T[x]
    row, col = iota((ROWS, ROWS), 0), iota((ROWS, ROWS), 1)
    turn = (((row >> 2) & 3) * 32 + (row >> 4) * 4 + (row & 3) == col).astype(BF16)
    for copy in in_x:
        copy.wait_recv()
    pl.semaphore_wait(ready, len(y_peers))
    turned = dot(turn, A[...].reshape(ROWS, HALF), PLAIN)
    C[...] = turned.astype(BF16).reshape(2 * NY, 16, HALF)

    in_z = [[] for _ in range(NY)]
    for dy, dz in plane:
        yt, zt = (y + dy) % NY, (z + dz) % NZ
        o = dy * NZ + dz
        in_z[dy].append(
            send(C.at[2 * yt + zt // SEG], DD.at[dy, dz], zs_s.at[o], zs_r.at[o], at(x, yt, zt))
        )
    DD[0, 0] = C[2 * y + zh]
    for copy in in_cx:
        copy.wait_recv()
    CY[0] = jnp.sum(CX[...], axis=0)
    in_cy = [send(CY.at[0], CY.at[k], cy_s.at[k], cy_r.at[k], y_peers[k - 1]) for k in range(1, NY)]

    for copy in in_src:
        copy.wait_recv()
    lane512 = iota((1, 512), 1)
    from_x, from_y = (x + NX - ((lane512 >> 2) & 3)) & 3, (y + NY - (lane512 >> 7)) & 3
    from_z = (z + NZ - ((lane512 >> 4) & 7)) & 7
    code = (((from_x * NY + from_y) * NZ + from_z) * SEG + (lane512 & 3)).astype(F32)
    place_iota = iota((ROWS, ROWS), 0).astype(F32)
    for b in range(SEG):
        block = SRC[b]
        wanted = jnp.transpose(block)[:, 0:1] * SEG + b
        PM[b * ROWS : (b + 1) * ROWS] = (wanted == code).astype(BF16)
        alive = place_iota < block[1:2]
        MKS[b * ROWS : (b + 1) * ROWS] = jnp.where(alive, 0.0, NEG).astype(BF16)
        AS[b] = (iota((ROWS, ROWS), 1).astype(F32) < block[1:2]).astype(BF16)
        QA[b, 0:ROWS, ROWS:] = (col == 0).astype(BF16)
        QA[b, ROWS:, ROWS:] = (col == 1).astype(BF16)
        M[b] = jnp.full((8, 256), NEG, F32)
        L[b] = jnp.zeros((8, 256), F32)
        O[b] = jnp.zeros((ROWS, 256), F32)
    out_row, from_row = iota((160, 512), 0), iota((160, 512), 1)
    for h in range(2):
        head = first_head + h
        mid = (out_row >> 5) * ROWS + (out_row & 31) * 4 + head % 4
        far_row = out_row - ROWS
        far = (far_row >> 3) * ROWS + (far_row & 7) * 16 + head
        select = (jnp.where(out_row < ROWS, mid, far) == from_row).astype(BF16)
        SEL[h] = dot(select, PM[...], PLAIN).astype(BF16)
    for copy in in_cy:
        copy.wait_recv()
    CZ[0] = jnp.sum(CY[...], axis=0)
    in_cz = [
        send(CZ.at[0], CZ.at[k], cz_s.at[k], cz_r.at[k], at(x, y, (z + k) % NZ))
        for k in range(1, NZ)
    ]
    for copy in weights:
        copy.wait()

    gain_mine = jnp.concatenate([gain[pl.ds(3 * core + i, 1)] for i in range(3)], axis=1)
    gain_other = jnp.concatenate([gain[pl.ds(3 - 3 * core + i, 1)] for i in range(3)], axis=1)
    w_mine = w_v[pl.ds(pl.multiple_of(core * HALF, HALF), HALF)]
    w_other = w_v[pl.ds(pl.multiple_of((1 - core) * HALF, HALF), HALF)]
    in_p = []

    def project(c):
        a = DD[c].reshape(ROWS, HALF).astype(F32)
        b = E[c].reshape(ROWS, HALF).astype(F32)
        mean = (jnp.sum(a, 1, keepdims=True) + jnp.sum(b, 1, keepdims=True)) / D
        a, b = a - mean, b - mean
        var = (jnp.sum(a * a, 1, keepdims=True) + jnp.sum(b * b, 1, keepdims=True)) / D
        scale = lax.rsqrt(var + 1e-05)
        a = (a * scale * gain_mine).astype(BF16)
        b = (b * scale * gain_other).astype(BF16)
        R[c * ROWS : (c + 1) * ROWS] = (dot(a, w_mine, PLAIN) + dot(b, w_other, PLAIN)).astype(BF16)

    for c in range(NY):
        for copy in in_z[c]:
            copy.wait_recv()
        in_p.append(send(DD.at[c], E.at[c], ps_s.at[c], ps_r.at[c], sibling))
        if c:
            in_p[c - 1].wait_recv()
            project(c - 1)
    in_p[NY - 1].wait_recv()
    project(NY - 1)

    low = (iota((1, 2 * ROWS), 1) & 127) < 64
    kv = R[:, ROWS:]
    picked = jnp.where(low, dot(SEL[0], kv, PLAIN), dot(SEL[1], kv, PLAIN)).astype(BF16)
    HM[0, 0, 0:ROWS] = picked[0:ROWS, 0:ROWS]
    HM[0, 0, ROWS:] = picked[0:ROWS, ROWS:]
    GF[0, 0, 0, 0:LONG] = picked[ROWS:, 0:ROWS]
    GF[0, 0, 0, LONG : 2 * LONG] = picked[ROWS:, ROWS:]

    def to_xy(f, o):
        dx, dy = o // NY, o % NY
        return send(
            GF.at[0, 0, f], GF.at[dx, dy, f], gf_s.at[2 * o + f], gf_r.at[2 * o + f],
            at((x + dx) % NX, (y + dy) % NY, z),
        )

    def middle(yy, f, source, device):
        o = 2 * yy + f
        return send(source, HM.at[yy, f], hm_s.at[o], hm_r.at[o], device)

    mirror, partner = at(x, y, NZ - 1 - z), at(x, y + 1 - 2 * (y % 2), z)
    order = (10, 11, 9, 14, 6, 2, 8, 3, 1, 12, 4, 7, 13, 15, 5)
    in_far = send(GF.at[0, 0, 0], GF.at[0, 0, 1], gf_s.at[1], gf_r.at[1], mirror)
    in_near = {o: to_xy(0, o) for o in order}
    in_m01 = middle(0, 1, HM.at[0, 0], mirror)
    in_m10 = middle(1, 0, HM.at[0, 0], partner)
    qkv = dot(PM[...], R[...], PLAIN)
    KS[...] = qkv[:, ROWS : 2 * ROWS].astype(BF16)
    VS[...] = qkv[:, 2 * ROWS :].astype(BF16)
    q32 = qkv[:, 0:ROWS].astype(BF16).astype(F32) * 0.125
    for b in range(SEG):
        q_b = q32[b * ROWS : (b + 1) * ROWS]
        QA[b, 0:ROWS, 0:ROWS] = jnp.where(col < 64, q_b, 0.0).astype(BF16)
        QA[b, ROWS:, 0:ROWS] = jnp.where(col < 64, 0.0, q_b).astype(BF16)

    def absorb(keys, values, masks, finish=None):
        keys = jnp.concatenate([keys, masks], axis=1)
        turned_values = jnp.transpose(values)
        blocks = range(SEG)
        scores = [dot(keys, QA[b], MINOR) for b in blocks]
        old = [M[b][0:1] for b in blocks]
        new = [jnp.maximum(old[b], jnp.max(scores[b], axis=0, keepdims=True)) for b in blocks]
        weight = [jnp.exp(scores[b] - new[b]) for b in blocks]
        rescale = [jnp.exp(old[b] - new[b]) for b in blocks]
        mixed = [dot(turned_values, weight[b].astype(BF16), PLAIN) for b in blocks]
        for b in blocks:
            total = L[b][0:1] * rescale[b] + jnp.sum(weight[b], axis=0, keepdims=True)
            O[b] = O[b] * rescale[b] + mixed[b]
            M[b] = jnp.broadcast_to(new[b], (8, 256))
            L[b] = jnp.broadcast_to(total, (8, 256))
            if finish is not None:
                finish(b)

    for copy in in_cz:
        copy.wait_recv()
    counts = jnp.broadcast_to(jnp.sum(CZ[...], axis=0)[0:1], (ROWS, ROWS)).astype(BF16)

    def mask(n, device, position, stride):
        owner = (device == iota((n, ROWS), 1)).astype(BF16)
        head = first_head + jnp.minimum(iota((n, ROWS), 1), 1)
        position = position * stride + head % stride
        alive = position.astype(F32) < dot(owner, counts, MINOR)
        return jnp.where(alive, 0.0, NEG).astype(BF16)

    def in_half(f, b):
        return SEG * (zh + f - 2 * zh * f) + b

    r = iota((512, ROWS), 0)
    device = (x * NY + (y ^ (r >> 8))) * NZ + in_half((r >> 7) & 1, (r >> 5) & 3)
    MKM[...] = mask(512, device, r & 31, 4)
    r = iota((1024, ROWS), 0)
    device = ((x + NX - ((r >> 7) & 3)) & 3) * NY + ((y + NY - ((r >> 5) & 3)) & 3)
    MKL[...] = mask(1024, device * NZ + in_half(r >> 9, (r >> 3) & 3), r & 7, 16)
    absorb(KS[...], VS[...], MKS[...])
    in_far.wait_recv()
    in_other = {o: to_xy(1, o) for o in order}
    in_m01.wait_recv()
    in_m11 = middle(1, 1, HM.at[0, 1], partner)

    for o in order:
        in_near[o].wait_recv()
    absorb(
        GF[:, :, 0, 0:LONG].reshape(512, ROWS),
        GF[:, :, 0, LONG:].reshape(512, ROWS),
        MKL[0:512],
    )
    in_m10.wait_recv()
    in_m11.wait_recv()
    absorb(
        HM[:, :, 0:ROWS].reshape(512, ROWS),
        HM[:, :, ROWS:].reshape(512, ROWS),
        MKM[...],
    )
    backs = []

    def give_back(b):
        halves = []
        for h in range(2):
            cols = slice(h * ROWS, (h + 1) * ROWS)
            halves.append(O[b][h * 64 : (h + 1) * 64, cols] / L[b][0:1, cols])
        AS[b] = (jnp.concatenate(halves, axis=0) * AS[b].astype(F32)).astype(BF16)
        target = b + zh * (SEG - 1 - 2 * b)
        here = (place == 1) | (place == 2)
        here = here | ((place == 0) & (target == 1)) | ((place == 3) & (target == 2))
        here = here & (place != target)
        copy = remote(AS.at[b], AT.at[pair], at_s.at[b], at_r.at[pair], at(x, y, SEG * zh + b))
        backs.append((copy, here))
        pl.when(here)(copy.start)

    for dx in (0, 2):
        for o in order:
            if o // NY in (dx, dx + 1):
                in_other[o].wait_recv()
        absorb(
            GF[dx : dx + 2, :, 1, 0:LONG].reshape(256, ROWS),
            GF[dx : dx + 2, :, 1, LONG:].reshape(256, ROWS),
            MKL[512 + 128 * dx : 768 + 128 * dx],
            give_back if dx else None,
        )
    AT[pair] = AS[zj]
    for g in range(3):
        arrival = remote(AS.at[0], AT.at[g], at_s.at[0], at_r.at[g], sibling)
        pl.when(pair != g)(arrival.wait_recv)
    attended = AT[...].reshape(HALF, ROWS)
    mine = pl.ds(pl.multiple_of(core * HALF, HALF), HALF)
    other = pl.ds(pl.multiple_of((1 - core) * HALF, HALF), HALF)
    PO[...] = dot(attended, w_out[:, other], MAJOR).astype(BF16)
    in_o = send(PO, other_part, o_s.at[0], o_r.at[0], sibling)
    OWN[...] = dot(attended, w_out[:, mine], MAJOR)
    hand_out = pltpu.make_async_copy(OWN, own_part, loc_sem.at[0])
    hand_out.start()
    hand_out.wait()
    in_o.wait_recv()
    for copy, here in backs:
        pl.when(here)(copy.wait_send)
    for copy in pending:
        copy.wait_send()


def shards(tiles, ln_gain, w_qkv, w_out, tile_source, tissue_count):
    dma = pltpu.SemaphoreType.DMA
    scratch = [
        pltpu.VMEM((D, 3 * ROWS), BF16),
        pltpu.VMEM((HALF, D), BF16),
        pltpu.VMEM((6, ROWS), F32),
        pltpu.VMEM((1, ROWS), jnp.int32),
        pltpu.SMEM((1,), jnp.int32),
        pltpu.VMEM((NX, 32, HALF), BF16),
        pltpu.VMEM((NX, 32, HALF), BF16),
        pltpu.VMEM((2 * NY, 16, HALF), BF16),
        pltpu.VMEM((NY, NZ, 16, HALF), BF16),
        pltpu.VMEM((NY, NZ, 16, HALF), BF16),
        pltpu.VMEM((SEG, 8, ROWS), F32),
        pltpu.VMEM((512, 3 * ROWS), BF16),
        pltpu.VMEM((512, 512), BF16),
        pltpu.VMEM((2, 160, 512), BF16),
        pltpu.VMEM((512, ROWS), BF16),
        pltpu.VMEM((512, ROWS), BF16),
        pltpu.VMEM((512, ROWS), BF16),
        pltpu.VMEM((512, ROWS), BF16),
        pltpu.VMEM((1024, ROWS), BF16),
        pltpu.VMEM((NX, 8, ROWS), F32),
        pltpu.VMEM((NY, 8, ROWS), F32),
        pltpu.VMEM((NZ, 8, ROWS), F32),
        pltpu.VMEM((NX, NY, 2, 64, ROWS), BF16),
        pltpu.VMEM((2, 2, 256, ROWS), BF16),
        pltpu.VMEM((SEG, 256, 256), BF16),
        pltpu.VMEM((SEG, 8, 256), F32),
        pltpu.VMEM((SEG, 8, 256), F32),
        pltpu.VMEM((SEG, ROWS, 256), F32),
        pltpu.VMEM((SEG, ROWS, ROWS), BF16),
        pltpu.VMEM((3, ROWS, ROWS), BF16),
        pltpu.VMEM((ROWS, HALF), BF16),
        pltpu.VMEM((ROWS, HALF), F32),
        dma((5,)), dma((3,)), pltpu.SemaphoreType.REGULAR,
    ]
    for size in (NX, NY * NZ, NY, SEG, NX * NY * 2, 4, SEG, 1, NX, NY, NZ):
        scratch += [dma((size,)), dma((size,))]
    anywhere = pl.BlockSpec(memory_space=pltpu.HBM)
    own_part, other_part = pl.pallas_call(
        kernel,
        out_shape=(
            jax.ShapeDtypeStruct((ROWS, HALF), F32),
            jax.ShapeDtypeStruct((ROWS, HALF), BF16),
        ),
        in_specs=[anywhere] * 6,
        out_specs=(anywhere, anywhere),
        scratch_shapes=scratch,
        compiler_params=pltpu.CompilerParams(
            collective_id=0, has_side_effects=True, vmem_limit_bytes=64 << 20
        ),
    )(
        tiles.reshape(NX, 32, HALF),
        ln_gain.reshape(6, ROWS),
        jnp.transpose(w_qkv, (1, 0, 2)),
        w_out,
        tile_source.reshape(1, ROWS),
        tissue_count,
    )
    return (own_part + other_part.astype(F32)).astype(BF16)


def solution(mesh):
    return jax.shard_map(
        shards,
        mesh=mesh,
        in_specs=(
            P("seq", "head"),
            P(),
            P(None, None, "head"),
            P("head", None),
            P("seq"),
            P("seq"),
        ),
        out_specs=P("seq", "head"),
        check_vma=False,
    )
```

```python
import jax
import jax.numpy as jnp
from jax import lax
from jax.experimental import pallas as pl
from jax.experimental.pallas import tpu as pltpu
from jax.sharding import PartitionSpec as P

D = 768
HALF = 384
ROWS = 128
NX, NY, NZ = 4, 4, 8
SEG = 4
LONG = SEG * 8
NEG = -1e30
F32 = jnp.float32
BF16 = jnp.bfloat16
MESH = pl.DeviceIdType.MESH
PLAIN = (((1,), (0,)), ((), ()))
MINOR = (((1,), (1,)), ((), ()))
MAJOR = (((0,), (0,)), ((), ()))


def iota(shape, dim):
    return lax.broadcasted_iota(jnp.int32, shape, dim)


def dot(a, b, dims):
    return lax.dot_general(a, b, dims, preferred_element_type=F32)


def kernel(
    tiles, gain_in, w_qkv, w_out_in, src_in, cnt_in,
    own_part, other_part,
    w_v, w_out, gain, src, cnt, T, A, C, DD, E, SRC, R, PM, SEL,
    KS, VS, MKS, MKM, MKL, CX, CY, CZ, GF, HM, QA, M, L, O, AS, AT, PO, OWN,
    w_sem, loc_sem, ready,
    xs_s, xs_r, zs_s, zs_r, ps_s, ps_r, src_s, src_r,
    gf_s, gf_r, hm_s, hm_r, at_s, at_r, o_s, o_r,
    cx_s, cx_r, cy_s, cy_r, cz_s, cz_r,
):
    seq = lax.axis_index("seq")
    core = lax.axis_index("head")
    x, y, z = seq // (NY * NZ), (seq // NZ) % NY, seq % NZ
    zh, zj = z // SEG, z % SEG
    place = zj + zh * (SEG - 1 - 2 * zj)
    pair = place % 3
    first_head = 6 * core + 2 * pair
    sibling = {"head": 1 - core}
    pending = []

    def at(px, py, pz):
        return {"seq": (px * NY + py) * NZ + pz}

    def remote(source, target, s_sem, r_sem, device):
        return pltpu.make_async_remote_copy(
            src_ref=source, dst_ref=target, send_sem=s_sem, recv_sem=r_sem,
            device_id=device, device_id_type=MESH,
        )

    def send(source, target, s_sem, r_sem, device):
        copy = remote(source, target, s_sem, r_sem, device)
        copy.start()
        pending.append(copy)
        return copy

    lanes = pl.ds(pl.multiple_of(pair * ROWS, ROWS), ROWS)
    weights = [
        pltpu.make_async_copy(w_qkv.at[t, :, lanes], w_v.at[:, t * ROWS : (t + 1) * ROWS], w_sem.at[t])
        for t in range(3)
    ]
    weights += [pltpu.make_async_copy(w_out_in, w_out, w_sem.at[3])]
    weights += [pltpu.make_async_copy(gain_in, gain, w_sem.at[4])]
    small = [
        pltpu.make_async_copy(src_in, src, loc_sem.at[1]),
        pltpu.make_async_copy(cnt_in, cnt, loc_sem.at[2]),
    ]
    own_t = pltpu.make_async_copy(tiles, T, loc_sem.at[0])
    barrier = pltpu.get_barrier_semaphore()
    peers = [at((x + k) % NX, y, z) for k in range(1, NX)] + [sibling]
    plane = [(o // NZ, o % NZ) for o in range(1, NY * NZ)]
    y_peers = [at(x, (y + k) % NY, z) for k in range(1, NY)]
    peers += y_peers + [at(x, y, (z + k) % NZ) for k in range(1, NZ)]
    for peer in peers:
        pl.semaphore_signal(barrier, inc=1, device_id=peer, device_id_type=MESH)
    for copy in small + [own_t] + weights:
        copy.start()
    for copy in small + [own_t]:
        copy.wait()
    own_count = cnt[0]
    rows8 = iota((8, ROWS), 0)
    tag = jnp.where(rows8 == 0, src[...] // ROWS, own_count)
    SRC[zj] = tag.astype(F32)
    CX[0] = jnp.where(iota((8, ROWS), 1) == seq, own_count, 0).astype(F32)
    pl.semaphore_wait(barrier, len(peers))
    for peer in y_peers:
        pl.semaphore_signal(ready, inc=1, device_id=peer, device_id_type=MESH)

    in_x = [
        send(T.at[(x + k) % NX], A.at[k], xs_s.at[k], xs_r.at[k], at((x + k) % NX, y, z))
        for k in range(1, NX)
    ]
    in_cx = [
        send(CX.at[0], CX.at[k], cx_s.at[k], cx_r.at[k], at((x + k) % NX, y, z))
        for k in range(1, NX)
    ]
    in_src = [
        send(SRC.at[zj], SRC.at[zj], src_s.at[t], src_r.at[t], at(x, y, SEG * zh + (zj + t) % SEG))
        for t in range(1, SEG)
    ]
    A[0] = T[x]
    row, col = iota((ROWS, ROWS), 0), iota((ROWS, ROWS), 1)
    turn = (((row >> 2) & 3) * 32 + (row >> 4) * 4 + (row & 3) == col).astype(BF16)
    for copy in in_x:
        copy.wait_recv()
    pl.semaphore_wait(ready, len(y_peers))
    turned = dot(turn, A[...].reshape(ROWS, HALF), PLAIN)
    C[...] = turned.astype(BF16).reshape(2 * NY, 16, HALF)

    in_z = [[] for _ in range(NY)]
    for dy, dz in plane:
        yt, zt = (y + dy) % NY, (z + dz) % NZ
        o = dy * NZ + dz
        in_z[dy].append(
            send(C.at[2 * yt + zt // SEG], DD.at[dy, dz], zs_s.at[o], zs_r.at[o], at(x, yt, zt))
        )
    DD[0, 0] = C[2 * y + zh]
    for copy in in_cx:
        copy.wait_recv()
    CY[0] = jnp.sum(CX[...], axis=0)
    in_cy = [send(CY.at[0], CY.at[k], cy_s.at[k], cy_r.at[k], y_peers[k - 1]) for k in range(1, NY)]

    for copy in in_src:
        copy.wait_recv()
    lane512 = iota((1, 512), 1)
    from_x, from_y = (x + NX - ((lane512 >> 2) & 3)) & 3, (y + NY - (lane512 >> 7)) & 3
    from_z = (z + NZ - ((lane512 >> 4) & 7)) & 7
    code = (((from_x * NY + from_y) * NZ + from_z) * SEG + (lane512 & 3)).astype(F32)
    place_iota = iota((ROWS, ROWS), 0).astype(F32)
    for b in range(SEG):
        block = SRC[b]
        wanted = jnp.transpose(block)[:, 0:1] * SEG + b
        PM[b * ROWS : (b + 1) * ROWS] = (wanted == code).astype(BF16)
        alive = place_iota < block[1:2]
        MKS[b * ROWS : (b + 1) * ROWS] = jnp.where(alive, 0.0, NEG).astype(BF16)
        QA[b, 0:ROWS, ROWS:] = (col == 0).astype(BF16)
        QA[b, ROWS:, ROWS:] = (col == 1).astype(BF16)
        M[b] = jnp.full((8, 256), NEG, F32)
        L[b] = jnp.zeros((8, 256), F32)
        O[b] = jnp.zeros((ROWS, 256), F32)
    out_row, from_row = iota((160, 512), 0), iota((160, 512), 1)
    for h in range(2):
        head = first_head + h
        mid = (out_row >> 5) * ROWS + (out_row & 31) * 4 + head % 4
        far_row = out_row - ROWS
        far = (far_row >> 3) * ROWS + (far_row & 7) * 16 + head
        select = (jnp.where(out_row < ROWS, mid, far) == from_row).astype(BF16)
        SEL[h] = dot(select, PM[...], PLAIN).astype(BF16)
    for copy in in_cy:
        copy.wait_recv()
    CZ[0] = jnp.sum(CY[...], axis=0)
    in_cz = [
        send(CZ.at[0], CZ.at[k], cz_s.at[k], cz_r.at[k], at(x, y, (z + k) % NZ))
        for k in range(1, NZ)
    ]
    for copy in weights:
        copy.wait()

    gain_mine = jnp.concatenate([gain[pl.ds(3 * core + i, 1)] for i in range(3)], axis=1)
    gain_other = jnp.concatenate([gain[pl.ds(3 - 3 * core + i, 1)] for i in range(3)], axis=1)
    w_mine = w_v[pl.ds(pl.multiple_of(core * HALF, HALF), HALF)]
    w_other = w_v[pl.ds(pl.multiple_of((1 - core) * HALF, HALF), HALF)]
    in_p = []

    def project(c):
        a = DD[c].reshape(ROWS, HALF).astype(F32)
        b = E[c].reshape(ROWS, HALF).astype(F32)
        mean = (jnp.sum(a, 1, keepdims=True) + jnp.sum(b, 1, keepdims=True)) / D
        a, b = a - mean, b - mean
        var = (jnp.sum(a * a, 1, keepdims=True) + jnp.sum(b * b, 1, keepdims=True)) / D
        scale = lax.rsqrt(var + 1e-05)
        a = (a * scale * gain_mine).astype(BF16)
        b = (b * scale * gain_other).astype(BF16)
        R[c * ROWS : (c + 1) * ROWS] = (dot(a, w_mine, PLAIN) + dot(b, w_other, PLAIN)).astype(BF16)

    for c in range(NY):
        for copy in in_z[c]:
            copy.wait_recv()
        in_p.append(send(DD.at[c], E.at[c], ps_s.at[c], ps_r.at[c], sibling))
        if c:
            in_p[c - 1].wait_recv()
            project(c - 1)
    in_p[NY - 1].wait_recv()
    project(NY - 1)

    low = (iota((1, 2 * ROWS), 1) & 127) < 64
    kv = R[:, ROWS:]
    picked = jnp.where(low, dot(SEL[0], kv, PLAIN), dot(SEL[1], kv, PLAIN)).astype(BF16)
    HM[0, 0, 0:ROWS] = picked[0:ROWS, 0:ROWS]
    HM[0, 0, ROWS:] = picked[0:ROWS, ROWS:]
    GF[0, 0, 0, 0:LONG] = picked[ROWS:, 0:ROWS]
    GF[0, 0, 0, LONG : 2 * LONG] = picked[ROWS:, ROWS:]

    def to_xy(f, o):
        dx, dy = o // NY, o % NY
        return send(
            GF.at[0, 0, f], GF.at[dx, dy, f], gf_s.at[2 * o + f], gf_r.at[2 * o + f],
            at((x + dx) % NX, (y + dy) % NY, z),
        )

    def middle(yy, f, source, device):
        o = 2 * yy + f
        return send(source, HM.at[yy, f], hm_s.at[o], hm_r.at[o], device)

    mirror, partner = at(x, y, NZ - 1 - z), at(x, y + 1 - 2 * (y % 2), z)
    order = (10, 11, 9, 14, 6, 2, 8, 3, 1, 12, 4, 7, 13, 15, 5)
    in_far = send(GF.at[0, 0, 0], GF.at[0, 0, 1], gf_s.at[1], gf_r.at[1], mirror)
    in_m01 = middle(0, 1, HM.at[0, 0], mirror)
    in_near = {o: to_xy(0, o) for o in order}
    in_m10 = middle(1, 0, HM.at[0, 0], partner)
    qkv = dot(PM[...], R[...], PLAIN)
    KS[...] = qkv[:, ROWS : 2 * ROWS].astype(BF16)
    VS[...] = qkv[:, 2 * ROWS :].astype(BF16)
    q32 = qkv[:, 0:ROWS].astype(BF16).astype(F32) * 0.125
    for b in range(SEG):
        q_b = q32[b * ROWS : (b + 1) * ROWS]
        QA[b, 0:ROWS, 0:ROWS] = jnp.where(col < 64, q_b, 0.0).astype(BF16)
        QA[b, ROWS:, 0:ROWS] = jnp.where(col < 64, 0.0, q_b).astype(BF16)

    def absorb(keys, values, masks, finish=None):
        keys = jnp.concatenate([keys, masks], axis=1)
        turned_values = jnp.transpose(values)
        blocks = range(SEG)
        scores = [dot(keys, QA[b], MINOR) for b in blocks]
        old = [M[b][0:1] for b in blocks]
        new = [jnp.maximum(old[b], jnp.max(scores[b], axis=0, keepdims=True)) for b in blocks]
        weight = [jnp.exp(scores[b] - new[b]) for b in blocks]
        rescale = [jnp.exp(old[b] - new[b]) for b in blocks]
        mixed = [dot(turned_values, weight[b].astype(BF16), PLAIN) for b in blocks]
        for b in blocks:
            total = L[b][0:1] * rescale[b] + jnp.sum(weight[b], axis=0, keepdims=True)
            O[b] = O[b] * rescale[b] + mixed[b]
            M[b] = jnp.broadcast_to(new[b], (8, 256))
            L[b] = jnp.broadcast_to(total, (8, 256))
            if finish is not None:
                finish(b)

    for copy in in_cz:
        copy.wait_recv()
    counts = jnp.broadcast_to(jnp.sum(CZ[...], axis=0)[0:1], (ROWS, ROWS)).astype(BF16)

    def mask(n, device, position, stride):
        owner = (device == iota((n, ROWS), 1)).astype(BF16)
        head = first_head + jnp.minimum(iota((n, ROWS), 1), 1)
        position = position * stride + head % stride
        alive = position.astype(F32) < dot(owner, counts, MINOR)
        return jnp.where(alive, 0.0, NEG).astype(BF16)

    def in_half(f, b):
        return SEG * (zh + f - 2 * zh * f) + b

    r = iota((512, ROWS), 0)
    device = (x * NY + (y ^ (r >> 8))) * NZ + in_half((r >> 7) & 1, (r >> 5) & 3)
    MKM[...] = mask(512, device, r & 31, 4)
    r = iota((1024, ROWS), 0)
    device = ((x + NX - ((r >> 7) & 3)) & 3) * NY + ((y + NY - ((r >> 5) & 3)) & 3)
    MKL[...] = mask(1024, device * NZ + in_half(r >> 9, (r >> 3) & 3), r & 7, 16)
    absorb(KS[...], VS[...], MKS[...])
    in_far.wait_recv()
    in_other = {o: to_xy(1, o) for o in order}
    in_m01.wait_recv()
    in_m11 = middle(1, 1, HM.at[0, 1], partner)

    for o in order:
        in_near[o].wait_recv()
    absorb(
        GF[:, :, 0, 0:LONG].reshape(512, ROWS),
        GF[:, :, 0, LONG:].reshape(512, ROWS),
        MKL[0:512],
    )
    in_m10.wait_recv()
    middles = [HM[0, 0], HM[0, 1], HM[1, 0]]
    absorb(
        jnp.concatenate([part[0:ROWS] for part in middles], axis=0),
        jnp.concatenate([part[ROWS:] for part in middles], axis=0),
        MKM[0:384],
    )
    backs = []
    alive_lanes = [
        (iota((1, ROWS), 1).astype(F32) < SRC[b][1:2]).astype(F32) for b in range(SEG)
    ]

    def give_back(b):
        halves = []
        for h in range(2):
            cols = slice(h * ROWS, (h + 1) * ROWS)
            scale = alive_lanes[b] / L[b][0:1, cols]
            halves.append(O[b][h * 64 : (h + 1) * 64, cols] * scale)
        AS[b] = jnp.concatenate(halves, axis=0).astype(BF16)
        target = b + zh * (SEG - 1 - 2 * b)
        here = (place == 1) | (place == 2)
        here = here | ((place == 0) & (target == 1)) | ((place == 3) & (target == 2))
        here = here & (place != target)
        copy = remote(AS.at[b], AT.at[pair], at_s.at[b], at_r.at[pair], at(x, y, SEG * zh + b))
        backs.append((copy, here))
        pl.when(here)(copy.start)

    for dx in (0, 2):
        for o in order:
            if o // NY in (dx, dx + 1):
                in_other[o].wait_recv()
        keys = GF[dx : dx + 2, :, 1, 0:LONG].reshape(256, ROWS)
        values = GF[dx : dx + 2, :, 1, LONG:].reshape(256, ROWS)
        masks = MKL[512 + 128 * dx : 768 + 128 * dx]
        if dx:
            in_m11.wait_recv()
            keys = jnp.concatenate([keys, HM[1, 1, 0:ROWS]], axis=0)
            values = jnp.concatenate([values, HM[1, 1, ROWS:]], axis=0)
            masks = jnp.concatenate([masks, MKM[384:]], axis=0)
        absorb(keys, values, masks, give_back if dx else None)
    AT[pair] = AS[zj]
    for copy in pending:
        copy.wait_send()
    mine = pl.ds(pl.multiple_of(core * HALF, HALF), HALF)
    other = pl.ds(pl.multiple_of((1 - core) * HALF, HALF), HALF)
    groups = [slice(g * ROWS, (g + 1) * ROWS) for g in range(3)]
    for_other = jnp.zeros((ROWS, HALF), F32)
    for g in range(3):
        arrival = remote(AS.at[0], AT.at[g], at_s.at[0], at_r.at[g], sibling)
        pl.when(pair != g)(arrival.wait_recv)
        for_other = for_other + dot(AT[g], w_out[groups[g], other], MAJOR)
    PO[...] = for_other.astype(BF16)
    in_o = remote(PO, other_part, o_s.at[0], o_r.at[0], sibling)
    in_o.start()
    OWN[...] = dot(AT[...].reshape(HALF, ROWS), w_out[:, mine], MAJOR)
    hand_out = pltpu.make_async_copy(OWN, own_part, loc_sem.at[0])
    hand_out.start()
    hand_out.wait()
    for copy, here in backs:
        pl.when(here)(copy.wait_send)
    in_o.wait()


def shards(tiles, ln_gain, w_qkv, w_out, tile_source, tissue_count):
    dma = pltpu.SemaphoreType.DMA
    scratch = [
        pltpu.VMEM((D, 3 * ROWS), BF16),
        pltpu.VMEM((HALF, D), BF16),
        pltpu.VMEM((6, ROWS), F32),
        pltpu.VMEM((1, ROWS), jnp.int32),
        pltpu.SMEM((1,), jnp.int32),
        pltpu.VMEM((NX, 32, HALF), BF16),
        pltpu.VMEM((NX, 32, HALF), BF16),
        pltpu.VMEM((2 * NY, 16, HALF), BF16),
        pltpu.VMEM((NY, NZ, 16, HALF), BF16),
        pltpu.VMEM((NY, NZ, 16, HALF), BF16),
        pltpu.VMEM((SEG, 8, ROWS), F32),
        pltpu.VMEM((512, 3 * ROWS), BF16),
        pltpu.VMEM((512, 512), BF16),
        pltpu.VMEM((2, 160, 512), BF16),
        pltpu.VMEM((512, ROWS), BF16),
        pltpu.VMEM((512, ROWS), BF16),
        pltpu.VMEM((512, ROWS), BF16),
        pltpu.VMEM((512, ROWS), BF16),
        pltpu.VMEM((1024, ROWS), BF16),
        pltpu.VMEM((NX, 8, ROWS), F32),
        pltpu.VMEM((NY, 8, ROWS), F32),
        pltpu.VMEM((NZ, 8, ROWS), F32),
        pltpu.VMEM((NX, NY, 2, 64, ROWS), BF16),
        pltpu.VMEM((2, 2, 256, ROWS), BF16),
        pltpu.VMEM((SEG, 256, 256), BF16),
        pltpu.VMEM((SEG, 8, 256), F32),
        pltpu.VMEM((SEG, 8, 256), F32),
        pltpu.VMEM((SEG, ROWS, 256), F32),
        pltpu.VMEM((SEG, ROWS, ROWS), BF16),
        pltpu.VMEM((3, ROWS, ROWS), BF16),
        pltpu.VMEM((ROWS, HALF), BF16),
        pltpu.VMEM((ROWS, HALF), F32),
        dma((5,)), dma((3,)), pltpu.SemaphoreType.REGULAR,
    ]
    for size in (NX, NY * NZ, NY, SEG, NX * NY * 2, 4, SEG, 1, NX, NY, NZ):
        scratch += [dma((size,)), dma((size,))]
    anywhere = pl.BlockSpec(memory_space=pltpu.HBM)
    own_part, other_part = pl.pallas_call(
        kernel,
        out_shape=(
            jax.ShapeDtypeStruct((ROWS, HALF), F32),
            jax.ShapeDtypeStruct((ROWS, HALF), BF16),
        ),
        in_specs=[anywhere] * 6,
        out_specs=(anywhere, anywhere),
        scratch_shapes=scratch,
        compiler_params=pltpu.CompilerParams(
            collective_id=0, has_side_effects=True, vmem_limit_bytes=64 << 20
        ),
    )(
        tiles.reshape(NX, 32, HALF),
        ln_gain.reshape(6, ROWS),
        jnp.transpose(w_qkv, (1, 0, 2)),
        w_out,
        tile_source.reshape(1, ROWS),
        tissue_count,
    )
    return (own_part + other_part.astype(F32)).astype(BF16)


def solution(mesh):
    return jax.shard_map(
        shards,
        mesh=mesh,
        in_specs=(
            P("seq", "head"),
            P(),
            P(None, None, "head"),
            P("head", None),
            P("seq"),
            P("seq"),
        ),
        out_specs=P("seq", "head"),
        check_vma=False,
    )
```

```python
import jax
import jax.numpy as jnp
from jax import lax
from jax.experimental import pallas as pl
from jax.experimental.pallas import tpu as pltpu
from jax.sharding import PartitionSpec as P

D = 768
HALF = 384
ROWS = 128
NX, NY, NZ = 4, 4, 8
SEG = 4
LONG = SEG * 8
NEG = -1e30
F32 = jnp.float32
BF16 = jnp.bfloat16
MESH = pl.DeviceIdType.MESH
PLAIN = (((1,), (0,)), ((), ()))
MINOR = (((1,), (1,)), ((), ()))
MAJOR = (((0,), (0,)), ((), ()))


def iota(shape, dim):
    return lax.broadcasted_iota(jnp.int32, shape, dim)


def dot(a, b, dims):
    return lax.dot_general(a, b, dims, preferred_element_type=F32)


def kernel(
    tiles, gain_in, w_qkv, w_out_in, src_in, cnt_in,
    own_part, other_part,
    w_v, w_out, gain, src, cnt, T, A, C, DD, E, SRC, R, PM, SEL,
    KS, VS, MKS, MKM, MKL, CX, CY, CZ, GF, HM, QA, M, L, O, AS, AT, PO, OWN,
    w_sem, loc_sem, ready,
    xs_s, xs_r, zs_s, zs_r, ps_s, ps_r, src_s, src_r,
    gf_s, gf_r, hm_s, hm_r, at_s, at_r, o_s, o_r,
    cx_s, cx_r, cy_s, cy_r, cz_s, cz_r,
):
    seq = lax.axis_index("seq")
    core = lax.axis_index("head")
    x, y, z = seq // (NY * NZ), (seq // NZ) % NY, seq % NZ
    zh, zj = z // SEG, z % SEG
    place = zj + zh * (SEG - 1 - 2 * zj)
    pair = place % 3
    first_head = 6 * core + 2 * pair
    sibling = {"head": 1 - core}
    pending = []

    def at(px, py, pz):
        return {"seq": (px * NY + py) * NZ + pz}

    def remote(source, target, s_sem, r_sem, device):
        return pltpu.make_async_remote_copy(
            src_ref=source, dst_ref=target, send_sem=s_sem, recv_sem=r_sem,
            device_id=device, device_id_type=MESH,
        )

    def send(source, target, s_sem, r_sem, device):
        copy = remote(source, target, s_sem, r_sem, device)
        copy.start()
        pending.append(copy)
        return copy

    lanes = pl.ds(pl.multiple_of(pair * ROWS, ROWS), ROWS)
    weights = [
        pltpu.make_async_copy(w_qkv.at[t, :, lanes], w_v.at[:, t * ROWS : (t + 1) * ROWS], w_sem.at[t])
        for t in range(3)
    ]
    weights += [pltpu.make_async_copy(w_out_in, w_out, w_sem.at[3])]
    weights += [pltpu.make_async_copy(gain_in, gain, w_sem.at[4])]
    small = [
        pltpu.make_async_copy(src_in, src, loc_sem.at[1]),
        pltpu.make_async_copy(cnt_in, cnt, loc_sem.at[2]),
    ]
    own_t = pltpu.make_async_copy(tiles, T, loc_sem.at[0])
    barrier = pltpu.get_barrier_semaphore()
    peers = [at((x + k) % NX, y, z) for k in range(1, NX)] + [sibling]
    plane = [(o // NZ, o % NZ) for o in range(1, NY * NZ)]
    y_peers = [at(x, (y + k) % NY, z) for k in range(1, NY)]
    peers += y_peers + [at(x, y, (z + k) % NZ) for k in range(1, NZ)]
    for peer in peers:
        pl.semaphore_signal(barrier, inc=1, device_id=peer, device_id_type=MESH)
    for copy in small + [own_t] + weights:
        copy.start()
    own_t.wait()
    pl.semaphore_wait(barrier, len(peers))

    in_x = [
        send(T.at[(x + k) % NX], A.at[k], xs_s.at[k], xs_r.at[k], at((x + k) % NX, y, z))
        for k in range(1, NX)
    ]
    for copy in small:
        copy.wait()
    own_count = cnt[0]
    rows8 = iota((8, ROWS), 0)
    tag = jnp.where(rows8 == 0, src[...] // ROWS, own_count)
    SRC[zj] = tag.astype(F32)
    CX[0] = jnp.where(iota((8, ROWS), 1) == seq, own_count, 0).astype(F32)
    for peer in y_peers:
        pl.semaphore_signal(ready, inc=1, device_id=peer, device_id_type=MESH)
    in_cx = [
        send(CX.at[0], CX.at[k], cx_s.at[k], cx_r.at[k], at((x + k) % NX, y, z))
        for k in range(1, NX)
    ]
    in_src = [
        send(SRC.at[zj], SRC.at[zj], src_s.at[t], src_r.at[t], at(x, y, SEG * zh + (zj + t) % SEG))
        for t in range(1, SEG)
    ]
    A[0] = T[x]
    row, col = iota((ROWS, ROWS), 0), iota((ROWS, ROWS), 1)
    turn = (((row >> 2) & 3) * 32 + (row >> 4) * 4 + (row & 3) == col).astype(BF16)
    for copy in in_x:
        copy.wait_recv()
    pl.semaphore_wait(ready, len(y_peers))
    turned = dot(turn, A[...].reshape(ROWS, HALF), PLAIN)
    C[...] = turned.astype(BF16).reshape(2 * NY, 16, HALF)

    in_z = [[] for _ in range(NY)]
    for dy, dz in plane:
        yt, zt = (y + dy) % NY, (z + dz) % NZ
        o = dy * NZ + dz
        in_z[dy].append(
            send(C.at[2 * yt + zt // SEG], DD.at[dy, dz], zs_s.at[o], zs_r.at[o], at(x, yt, zt))
        )
    DD[0, 0] = C[2 * y + zh]
    for copy in in_cx:
        copy.wait_recv()
    CY[0] = jnp.sum(CX[...], axis=0)
    in_cy = [send(CY.at[0], CY.at[k], cy_s.at[k], cy_r.at[k], y_peers[k - 1]) for k in range(1, NY)]

    for copy in in_src:
        copy.wait_recv()
    lane512 = iota((1, 512), 1)
    from_x, from_y = (x + NX - ((lane512 >> 2) & 3)) & 3, (y + NY - (lane512 >> 7)) & 3
    from_z = (z + NZ - ((lane512 >> 4) & 7)) & 7
    code = (((from_x * NY + from_y) * NZ + from_z) * SEG + (lane512 & 3)).astype(F32)
    place_iota = iota((ROWS, ROWS), 0).astype(F32)
    for b in range(SEG):
        block = SRC[b]
        wanted = jnp.transpose(block)[:, 0:1] * SEG + b
        PM[b * ROWS : (b + 1) * ROWS] = (wanted == code).astype(BF16)
        alive = place_iota < block[1:2]
        MKS[b * ROWS : (b + 1) * ROWS] = jnp.where(alive, 0.0, NEG).astype(BF16)
        QA[b, 0:ROWS, ROWS:] = (col == 0).astype(BF16)
        QA[b, ROWS:, ROWS:] = (col == 1).astype(BF16)
        M[b] = jnp.full((8, 256), NEG, F32)
        L[b] = jnp.zeros((8, 256), F32)
        O[b] = jnp.zeros((ROWS, 256), F32)
    out_row, from_row = iota((160, 512), 0), iota((160, 512), 1)
    for h in range(2):
        head = first_head + h
        mid = (out_row >> 5) * ROWS + (out_row & 31) * 4 + head % 4
        far_row = out_row - ROWS
        far = (far_row >> 3) * ROWS + (far_row & 7) * 16 + head
        select = (jnp.where(out_row < ROWS, mid, far) == from_row).astype(BF16)
        SEL[h] = dot(select, PM[...], PLAIN).astype(BF16)
    for copy in weights:
        copy.wait()

    gain_mine = jnp.concatenate([gain[pl.ds(3 * core + i, 1)] for i in range(3)], axis=1)
    gain_other = jnp.concatenate([gain[pl.ds(3 - 3 * core + i, 1)] for i in range(3)], axis=1)
    w_mine = w_v[pl.ds(pl.multiple_of(core * HALF, HALF), HALF)]
    w_other = w_v[pl.ds(pl.multiple_of((1 - core) * HALF, HALF), HALF)]
    in_p = []

    def project(c):
        a = DD[c].reshape(ROWS, HALF).astype(F32)
        b = E[c].reshape(ROWS, HALF).astype(F32)
        mean = (jnp.sum(a, 1, keepdims=True) + jnp.sum(b, 1, keepdims=True)) / D
        a, b = a - mean, b - mean
        var = (jnp.sum(a * a, 1, keepdims=True) + jnp.sum(b * b, 1, keepdims=True)) / D
        scale = lax.rsqrt(var + 1e-05)
        a = (a * scale * gain_mine).astype(BF16)
        b = (b * scale * gain_other).astype(BF16)
        R[c * ROWS : (c + 1) * ROWS] = (dot(a, w_mine, PLAIN) + dot(b, w_other, PLAIN)).astype(BF16)

    for c in range(NY):
        for copy in in_z[c]:
            copy.wait_recv()
        in_p.append(send(DD.at[c], E.at[c], ps_s.at[c], ps_r.at[c], sibling))
        if c:
            in_p[c - 1].wait_recv()
            project(c - 1)
        if c == 1:
            for copy in in_cy:
                copy.wait_recv()
            CZ[0] = jnp.sum(CY[...], axis=0)
            in_cz = [
                send(CZ.at[0], CZ.at[k], cz_s.at[k], cz_r.at[k], at(x, y, (z + k) % NZ))
                for k in range(1, NZ)
            ]
    in_p[NY - 1].wait_recv()
    project(NY - 1)

    low = (iota((1, 2 * ROWS), 1) & 127) < 64
    kv = R[:, ROWS:]
    picked = jnp.where(low, dot(SEL[0], kv, PLAIN), dot(SEL[1], kv, PLAIN)).astype(BF16)
    HM[0, 0, 0:ROWS] = picked[0:ROWS, 0:ROWS]
    HM[0, 0, ROWS:] = picked[0:ROWS, ROWS:]
    GF[0, 0, 0, 0:LONG] = picked[ROWS:, 0:ROWS]
    GF[0, 0, 0, LONG : 2 * LONG] = picked[ROWS:, ROWS:]

    def to_xy(f, o):
        dx, dy = o // NY, o % NY
        return send(
            GF.at[0, 0, f], GF.at[dx, dy, f], gf_s.at[2 * o + f], gf_r.at[2 * o + f],
            at((x + dx) % NX, (y + dy) % NY, z),
        )

    def middle(yy, f, source, device):
        o = 2 * yy + f
        return send(source, HM.at[yy, f], hm_s.at[o], hm_r.at[o], device)

    mirror, partner = at(x, y, NZ - 1 - z), at(x, y + 1 - 2 * (y % 2), z)
    order = (10, 11, 9, 14, 6, 2, 8, 3, 1, 12, 4, 7, 13, 15, 5)
    in_far = send(GF.at[0, 0, 0], GF.at[0, 0, 1], gf_s.at[1], gf_r.at[1], mirror)
    in_m01 = middle(0, 1, HM.at[0, 0], mirror)
    in_near = {o: to_xy(0, o) for o in order}
    in_m10 = middle(1, 0, HM.at[0, 0], partner)
    qkv = dot(PM[...], R[...], PLAIN)
    KS[...] = qkv[:, ROWS : 2 * ROWS].astype(BF16)
    VS[...] = qkv[:, 2 * ROWS :].astype(BF16)
    q32 = qkv[:, 0:ROWS].astype(BF16).astype(F32) * 0.125
    for b in range(SEG):
        q_b = q32[b * ROWS : (b + 1) * ROWS]
        QA[b, 0:ROWS, 0:ROWS] = jnp.where(col < 64, q_b, 0.0).astype(BF16)
        QA[b, ROWS:, 0:ROWS] = jnp.where(col < 64, 0.0, q_b).astype(BF16)

    def absorb(keys, values, masks, finish=None):
        keys = jnp.concatenate([keys, masks], axis=1)
        turned_values = jnp.transpose(values)
        blocks = range(SEG)
        scores = [dot(keys, QA[b], MINOR) for b in blocks]
        old = [M[b][0:1] for b in blocks]
        new = [jnp.maximum(old[b], jnp.max(scores[b], axis=0, keepdims=True)) for b in blocks]
        weight = [jnp.exp(scores[b] - new[b]) for b in blocks]
        rescale = [jnp.exp(old[b] - new[b]) for b in blocks]
        mixed = [dot(turned_values, weight[b].astype(BF16), PLAIN) for b in blocks]
        for b in blocks:
            total = L[b][0:1] * rescale[b] + jnp.sum(weight[b], axis=0, keepdims=True)
            O[b] = O[b] * rescale[b] + mixed[b]
            M[b] = jnp.broadcast_to(new[b], (8, 256))
            L[b] = jnp.broadcast_to(total, (8, 256))
            if finish is not None:
                finish(b)

    absorb(KS[...], VS[...], MKS[...])
    in_far.wait_recv()
    in_other = {o: to_xy(1, o) for o in order}
    for copy in in_cz:
        copy.wait_recv()
    counts = jnp.broadcast_to(jnp.sum(CZ[...], axis=0)[0:1], (ROWS, ROWS)).astype(BF16)

    def mask(n, device, position, stride):
        owner = (device == iota((n, ROWS), 1)).astype(BF16)
        head = first_head + jnp.minimum(iota((n, ROWS), 1), 1)
        position = position * stride + head % stride
        alive = position.astype(F32) < dot(owner, counts, MINOR)
        return jnp.where(alive, 0.0, NEG).astype(BF16)

    def in_half(f, b):
        return SEG * (zh + f - 2 * zh * f) + b

    r = iota((512, ROWS), 0)
    device = (x * NY + (y ^ (r >> 8))) * NZ + in_half((r >> 7) & 1, (r >> 5) & 3)
    MKM[...] = mask(512, device, r & 31, 4)
    r = iota((1024, ROWS), 0)
    device = ((x + NX - ((r >> 7) & 3)) & 3) * NY + ((y + NY - ((r >> 5) & 3)) & 3)
    MKL[...] = mask(1024, device * NZ + in_half(r >> 9, (r >> 3) & 3), r & 7, 16)
    in_m01.wait_recv()
    in_m11 = middle(1, 1, HM.at[0, 1], partner)

    for o in order:
        in_near[o].wait_recv()
    absorb(
        GF[:, :, 0, 0:LONG].reshape(512, ROWS),
        GF[:, :, 0, LONG:].reshape(512, ROWS),
        MKL[0:512],
    )
    in_m10.wait_recv()
    middles = [HM[0, 0], HM[0, 1], HM[1, 0]]
    absorb(
        jnp.concatenate([part[0:ROWS] for part in middles], axis=0),
        jnp.concatenate([part[ROWS:] for part in middles], axis=0),
        MKM[0:384],
    )
    backs = []
    alive_lanes = [
        (iota((1, ROWS), 1).astype(F32) < SRC[b][1:2]).astype(F32) for b in range(SEG)
    ]

    def give_back(b):
        halves = []
        for h in range(2):
            cols = slice(h * ROWS, (h + 1) * ROWS)
            scale = alive_lanes[b] / L[b][0:1, cols]
            halves.append(O[b][h * 64 : (h + 1) * 64, cols] * scale)
        AS[b] = jnp.concatenate(halves, axis=0).astype(BF16)
        target = b + zh * (SEG - 1 - 2 * b)
        here = (place == 1) | (place == 2)
        here = here | ((place == 0) & (target == 1)) | ((place == 3) & (target == 2))
        here = here & (place != target)
        copy = remote(AS.at[b], AT.at[pair], at_s.at[b], at_r.at[pair], at(x, y, SEG * zh + b))
        backs.append((copy, here))
        pl.when(here)(copy.start)

    for dx in (0, 2):
        for o in order:
            if o // NY in (dx, dx + 1):
                in_other[o].wait_recv()
        keys = GF[dx : dx + 2, :, 1, 0:LONG].reshape(256, ROWS)
        values = GF[dx : dx + 2, :, 1, LONG:].reshape(256, ROWS)
        masks = MKL[512 + 128 * dx : 768 + 128 * dx]
        if dx:
            in_m11.wait_recv()
            keys = jnp.concatenate([keys, HM[1, 1, 0:ROWS]], axis=0)
            values = jnp.concatenate([values, HM[1, 1, ROWS:]], axis=0)
            masks = jnp.concatenate([masks, MKM[384:]], axis=0)
        absorb(keys, values, masks, give_back if dx else None)
    AT[pair] = AS[zj]
    for copy in pending:
        copy.wait_send()
    mine = pl.ds(pl.multiple_of(core * HALF, HALF), HALF)
    other = pl.ds(pl.multiple_of((1 - core) * HALF, HALF), HALF)
    groups = [slice(g * ROWS, (g + 1) * ROWS) for g in range(3)]
    for_other = jnp.zeros((ROWS, HALF), F32)
    for g in range(3):
        arrival = remote(AS.at[0], AT.at[g], at_s.at[0], at_r.at[g], sibling)
        pl.when(pair != g)(arrival.wait_recv)
        for_other = for_other + dot(AT[g], w_out[groups[g], other], MAJOR)
    PO[...] = for_other.astype(BF16)
    in_o = remote(PO, other_part, o_s.at[0], o_r.at[0], sibling)
    in_o.start()
    OWN[...] = dot(AT[...].reshape(HALF, ROWS), w_out[:, mine], MAJOR)
    hand_out = pltpu.make_async_copy(OWN, own_part, loc_sem.at[0])
    hand_out.start()
    hand_out.wait()
    for copy, here in backs:
        pl.when(here)(copy.wait_send)
    in_o.wait()


def shards(tiles, ln_gain, w_qkv, w_out, tile_source, tissue_count):
    dma = pltpu.SemaphoreType.DMA
    scratch = [
        pltpu.VMEM((D, 3 * ROWS), BF16),
        pltpu.VMEM((HALF, D), BF16),
        pltpu.VMEM((6, ROWS), F32),
        pltpu.VMEM((1, ROWS), jnp.int32),
        pltpu.SMEM((1,), jnp.int32),
        pltpu.VMEM((NX, 32, HALF), BF16),
        pltpu.VMEM((NX, 32, HALF), BF16),
        pltpu.VMEM((2 * NY, 16, HALF), BF16),
        pltpu.VMEM((NY, NZ, 16, HALF), BF16),
        pltpu.VMEM((NY, NZ, 16, HALF), BF16),
        pltpu.VMEM((SEG, 8, ROWS), F32),
        pltpu.VMEM((512, 3 * ROWS), BF16),
        pltpu.VMEM((512, 512), BF16),
        pltpu.VMEM((2, 160, 512), BF16),
        pltpu.VMEM((512, ROWS), BF16),
        pltpu.VMEM((512, ROWS), BF16),
        pltpu.VMEM((512, ROWS), BF16),
        pltpu.VMEM((512, ROWS), BF16),
        pltpu.VMEM((1024, ROWS), BF16),
        pltpu.VMEM((NX, 8, ROWS), F32),
        pltpu.VMEM((NY, 8, ROWS), F32),
        pltpu.VMEM((NZ, 8, ROWS), F32),
        pltpu.VMEM((NX, NY, 2, 64, ROWS), BF16),
        pltpu.VMEM((2, 2, 256, ROWS), BF16),
        pltpu.VMEM((SEG, 256, 256), BF16),
        pltpu.VMEM((SEG, 8, 256), F32),
        pltpu.VMEM((SEG, 8, 256), F32),
        pltpu.VMEM((SEG, ROWS, 256), F32),
        pltpu.VMEM((SEG, ROWS, ROWS), BF16),
        pltpu.VMEM((3, ROWS, ROWS), BF16),
        pltpu.VMEM((ROWS, HALF), BF16),
        pltpu.VMEM((ROWS, HALF), F32),
        dma((5,)), dma((3,)), pltpu.SemaphoreType.REGULAR,
    ]
    for size in (NX, NY * NZ, NY, SEG, NX * NY * 2, 4, SEG, 1, NX, NY, NZ):
        scratch += [dma((size,)), dma((size,))]
    anywhere = pl.BlockSpec(memory_space=pltpu.HBM)
    own_part, other_part = pl.pallas_call(
        kernel,
        out_shape=(
            jax.ShapeDtypeStruct((ROWS, HALF), F32),
            jax.ShapeDtypeStruct((ROWS, HALF), BF16),
        ),
        in_specs=[anywhere] * 6,
        out_specs=(anywhere, anywhere),
        scratch_shapes=scratch,
        compiler_params=pltpu.CompilerParams(
            collective_id=0, has_side_effects=True, vmem_limit_bytes=64 << 20
        ),
    )(
        tiles.reshape(NX, 32, HALF),
        ln_gain.reshape(6, ROWS),
        jnp.transpose(w_qkv, (1, 0, 2)),
        w_out,
        tile_source.reshape(1, ROWS),
        tissue_count,
    )
    return (own_part + other_part.astype(F32)).astype(BF16)


def solution(mesh):
    return jax.shard_map(
        shards,
        mesh=mesh,
        in_specs=(
            P("seq", "head"),
            P(),
            P(None, None, "head"),
            P("head", None),
            P("seq"),
            P("seq"),
        ),
        out_specs=P("seq", "head"),
        check_vma=False,
    )
```

```python
import jax
import jax.numpy as jnp
from jax import lax
from jax.experimental import pallas as pl
from jax.experimental.pallas import tpu as pltpu
from jax.sharding import PartitionSpec as P

D = 768
HALF = 384
ROWS = 128
NX, NY, NZ = 4, 4, 8
SEG = 4
LONG = SEG * 8
NEG = -1e30
F32 = jnp.float32
BF16 = jnp.bfloat16
MESH = pl.DeviceIdType.MESH
PLAIN = (((1,), (0,)), ((), ()))
MINOR = (((1,), (1,)), ((), ()))
MAJOR = (((0,), (0,)), ((), ()))


def iota(shape, dim):
    return lax.broadcasted_iota(jnp.int32, shape, dim)


def dot(a, b, dims):
    return lax.dot_general(a, b, dims, preferred_element_type=F32)


def kernel(
    tiles, gain_in, w_qkv, w_out_in, src_in, cnt_in,
    own_part, other_part,
    w_v, w_out, gain, src, cnt, T, A, C, DD, E, SRC, R, PM, SEL,
    KS, VS, MKS, MKM, MKL, CX, CY, CZ, GF, HM, QA, M, L, O, AS, AT, PO, OWN,
    w_sem, loc_sem, ready,
    xs_s, xs_r, zs_s, zs_r, ps_s, ps_r, src_s, src_r,
    gf_s, gf_r, hm_s, hm_r, at_s, at_r, o_s, o_r,
    cx_s, cx_r, cy_s, cy_r, cz_s, cz_r,
):
    seq = lax.axis_index("seq")
    core = lax.axis_index("head")
    x, y, z = seq // (NY * NZ), (seq // NZ) % NY, seq % NZ
    zh, zj = z // SEG, z % SEG
    place = zj + zh * (SEG - 1 - 2 * zj)
    pair = place % 3
    first_head = 6 * core + 2 * pair
    sibling = {"head": 1 - core}
    pending = []

    def at(px, py, pz):
        return {"seq": (px * NY + py) * NZ + pz}

    def remote(source, target, s_sem, r_sem, device):
        return pltpu.make_async_remote_copy(
            src_ref=source, dst_ref=target, send_sem=s_sem, recv_sem=r_sem,
            device_id=device, device_id_type=MESH,
        )

    def send(source, target, s_sem, r_sem, device):
        copy = remote(source, target, s_sem, r_sem, device)
        copy.start()
        pending.append(copy)
        return copy

    lanes = pl.ds(pl.multiple_of(pair * ROWS, ROWS), ROWS)
    weights = [
        pltpu.make_async_copy(w_qkv.at[t, :, lanes], w_v.at[:, t * ROWS : (t + 1) * ROWS], w_sem.at[t])
        for t in range(3)
    ]
    weights += [pltpu.make_async_copy(w_out_in, w_out, w_sem.at[3])]
    weights += [pltpu.make_async_copy(gain_in, gain, w_sem.at[4])]
    small = [
        pltpu.make_async_copy(src_in, src, loc_sem.at[1]),
        pltpu.make_async_copy(cnt_in, cnt, loc_sem.at[2]),
    ]
    own_t = pltpu.make_async_copy(tiles, T, loc_sem.at[0])
    barrier = pltpu.get_barrier_semaphore()
    peers = [at((x + k) % NX, y, z) for k in range(1, NX)] + [sibling]
    plane = [(dy, dz) for dy in (2, 1, 3, 0) for dz in (4, 3, 5, 2, 6, 1, 7, 0) if dy or dz]
    y_peers = [at(x, (y + k) % NY, z) for k in range(1, NY)]
    peers += y_peers + [at(x, y, (z + k) % NZ) for k in range(1, NZ)]
    for peer in peers:
        pl.semaphore_signal(barrier, inc=1, device_id=peer, device_id_type=MESH)
    for copy in small + [own_t] + weights:
        copy.start()
    own_t.wait()
    pl.semaphore_wait(barrier, len(peers))

    in_x = [
        send(T.at[(x + k) % NX], A.at[k], xs_s.at[k], xs_r.at[k], at((x + k) % NX, y, z))
        for k in range(1, NX)
    ]
    for copy in small:
        copy.wait()
    own_count = cnt[0]
    rows8 = iota((8, ROWS), 0)
    tag = jnp.where(rows8 == 0, src[...] // ROWS, own_count)
    SRC[zj] = tag.astype(F32)
    CX[0] = jnp.where(iota((8, ROWS), 1) == seq, own_count, 0).astype(F32)
    for peer in y_peers:
        pl.semaphore_signal(ready, inc=1, device_id=peer, device_id_type=MESH)
    in_cx = [
        send(CX.at[0], CX.at[k], cx_s.at[k], cx_r.at[k], at((x + k) % NX, y, z))
        for k in range(1, NX)
    ]
    in_src = [
        send(SRC.at[zj], SRC.at[zj], src_s.at[t], src_r.at[t], at(x, y, SEG * zh + (zj + t) % SEG))
        for t in range(1, SEG)
    ]
    A[0] = T[x]
    row, col = iota((ROWS, ROWS), 0), iota((ROWS, ROWS), 1)
    turn = (((row >> 2) & 3) * 32 + (row >> 4) * 4 + (row & 3) == col).astype(BF16)
    for copy in in_x:
        copy.wait_recv()
    pl.semaphore_wait(ready, len(y_peers))
    turned = dot(turn, A[...].reshape(ROWS, HALF), PLAIN)
    C[...] = turned.astype(BF16).reshape(2 * NY, 16, HALF)

    in_z = [[] for _ in range(NY)]
    for dy, dz in plane:
        yt, zt = (y + dy) % NY, (z + dz) % NZ
        o = dy * NZ + dz
        in_z[dy].append(
            send(C.at[2 * yt + zt // SEG], DD.at[dy, dz], zs_s.at[o], zs_r.at[o], at(x, yt, zt))
        )
    DD[0, 0] = C[2 * y + zh]
    for copy in in_cx:
        copy.wait_recv()
    CY[0] = jnp.sum(CX[...], axis=0)
    in_cy = [send(CY.at[0], CY.at[k], cy_s.at[k], cy_r.at[k], y_peers[k - 1]) for k in range(1, NY)]

    for copy in in_src:
        copy.wait_recv()
    lane512 = iota((1, 512), 1)
    from_x, from_y = (x + NX - ((lane512 >> 2) & 3)) & 3, (y + NY - (lane512 >> 7)) & 3
    from_z = (z + NZ - ((lane512 >> 4) & 7)) & 7
    code = (((from_x * NY + from_y) * NZ + from_z) * SEG + (lane512 & 3)).astype(F32)
    place_iota = iota((ROWS, ROWS), 0).astype(F32)
    for b in range(SEG):
        block = SRC[b]
        wanted = jnp.transpose(block)[:, 0:1] * SEG + b
        PM[b * ROWS : (b + 1) * ROWS] = (wanted == code).astype(BF16)
        alive = place_iota < block[1:2]
        MKS[b * ROWS : (b + 1) * ROWS] = jnp.where(alive, 0.0, NEG).astype(BF16)
        QA[b, 0:ROWS, ROWS:] = (col == 0).astype(BF16)
        QA[b, ROWS:, ROWS:] = (col == 1).astype(BF16)
        M[b] = jnp.full((8, 256), NEG, F32)
        L[b] = jnp.zeros((8, 256), F32)
        O[b] = jnp.zeros((ROWS, 256), F32)
    out_row, from_row = iota((160, 512), 0), iota((160, 512), 1)
    for h in range(2):
        head = first_head + h
        mid = (out_row >> 5) * ROWS + (out_row & 31) * 4 + head % 4
        far_row = out_row - ROWS
        far = (far_row >> 3) * ROWS + (far_row & 7) * 16 + head
        select = (jnp.where(out_row < ROWS, mid, far) == from_row).astype(BF16)
        SEL[h] = dot(select, PM[...], PLAIN).astype(BF16)
    for copy in weights:
        copy.wait()

    gain_mine = jnp.concatenate([gain[pl.ds(3 * core + i, 1)] for i in range(3)], axis=1)
    gain_other = jnp.concatenate([gain[pl.ds(3 - 3 * core + i, 1)] for i in range(3)], axis=1)
    w_mine = w_v[pl.ds(pl.multiple_of(core * HALF, HALF), HALF)]
    w_other = w_v[pl.ds(pl.multiple_of((1 - core) * HALF, HALF), HALF)]

    def project(c):
        a = DD[c].reshape(ROWS, HALF).astype(F32)
        b = E[c].reshape(ROWS, HALF).astype(F32)
        mean = (jnp.sum(a, 1, keepdims=True) + jnp.sum(b, 1, keepdims=True)) / D
        a, b = a - mean, b - mean
        var = (jnp.sum(a * a, 1, keepdims=True) + jnp.sum(b * b, 1, keepdims=True)) / D
        scale = lax.rsqrt(var + 1e-05)
        a = (a * scale * gain_mine).astype(BF16)
        b = (b * scale * gain_other).astype(BF16)
        R[c * ROWS : (c + 1) * ROWS] = (dot(a, w_mine, PLAIN) + dot(b, w_other, PLAIN)).astype(BF16)

    turns = (2, 1, 3, 0)
    in_p = {}
    for i, c in enumerate(turns):
        for copy in in_z[c]:
            copy.wait_recv()
        in_p[c] = send(DD.at[c], E.at[c], ps_s.at[c], ps_r.at[c], sibling)
        if i:
            in_p[turns[i - 1]].wait_recv()
            project(turns[i - 1])
        if i == 1:
            for copy in in_cy:
                copy.wait_recv()
            CZ[0] = jnp.sum(CY[...], axis=0)
            in_cz = [
                send(CZ.at[0], CZ.at[k], cz_s.at[k], cz_r.at[k], at(x, y, (z + k) % NZ))
                for k in range(1, NZ)
            ]
    in_p[turns[-1]].wait_recv()
    project(turns[-1])

    low = (iota((1, 2 * ROWS), 1) & 127) < 64
    kv = R[:, ROWS:]
    picked = jnp.where(low, dot(SEL[0], kv, PLAIN), dot(SEL[1], kv, PLAIN)).astype(BF16)
    HM[0, 0, 0:ROWS] = picked[0:ROWS, 0:ROWS]
    HM[0, 0, ROWS:] = picked[0:ROWS, ROWS:]
    GF[0, 0, 0, 0:LONG] = picked[ROWS:, 0:ROWS]
    GF[0, 0, 0, LONG : 2 * LONG] = picked[ROWS:, ROWS:]

    def to_xy(f, o):
        dx, dy = o // NY, o % NY
        return send(
            GF.at[0, 0, f], GF.at[dx, dy, f], gf_s.at[2 * o + f], gf_r.at[2 * o + f],
            at((x + dx) % NX, (y + dy) % NY, z),
        )

    def middle(yy, f, source, device):
        o = 2 * yy + f
        return send(source, HM.at[yy, f], hm_s.at[o], hm_r.at[o], device)

    mirror, partner = at(x, y, NZ - 1 - z), at(x, y + 1 - 2 * (y % 2), z)
    order = (10, 11, 9, 14, 6, 2, 8, 3, 1, 12, 4, 7, 13, 15, 5)
    in_far = send(GF.at[0, 0, 0], GF.at[0, 0, 1], gf_s.at[1], gf_r.at[1], mirror)
    in_m01 = middle(0, 1, HM.at[0, 0], mirror)
    in_near = {o: to_xy(0, o) for o in order}
    in_m10 = middle(1, 0, HM.at[0, 0], partner)
    qkv = dot(PM[...], R[...], PLAIN)
    KS[...] = qkv[:, ROWS : 2 * ROWS].astype(BF16)
    VS[...] = qkv[:, 2 * ROWS :].astype(BF16)
    q32 = qkv[:, 0:ROWS].astype(BF16).astype(F32) * 0.125
    for b in range(SEG):
        q_b = q32[b * ROWS : (b + 1) * ROWS]
        QA[b, 0:ROWS, 0:ROWS] = jnp.where(col < 64, q_b, 0.0).astype(BF16)
        QA[b, ROWS:, 0:ROWS] = jnp.where(col < 64, 0.0, q_b).astype(BF16)

    def absorb(keys, values, masks, finish=None):
        keys = jnp.concatenate([keys, masks], axis=1)
        turned_values = jnp.transpose(values)
        blocks = range(SEG)
        scores = [dot(keys, QA[b], MINOR) for b in blocks]
        old = [M[b][0:1] for b in blocks]
        new = [jnp.maximum(old[b], jnp.max(scores[b], axis=0, keepdims=True)) for b in blocks]
        weight = [jnp.exp(scores[b] - new[b]) for b in blocks]
        rescale = [jnp.exp(old[b] - new[b]) for b in blocks]
        mixed = [dot(turned_values, weight[b].astype(BF16), PLAIN) for b in blocks]
        for b in blocks:
            total = L[b][0:1] * rescale[b] + jnp.sum(weight[b], axis=0, keepdims=True)
            O[b] = O[b] * rescale[b] + mixed[b]
            M[b] = jnp.broadcast_to(new[b], (8, 256))
            L[b] = jnp.broadcast_to(total, (8, 256))
            if finish is not None:
                finish(b)

    absorb(KS[...], VS[...], MKS[...])
    in_far.wait_recv()
    in_other = {o: to_xy(1, o) for o in order}
    for copy in in_cz:
        copy.wait_recv()
    counts = jnp.broadcast_to(jnp.sum(CZ[...], axis=0)[0:1], (ROWS, ROWS)).astype(BF16)

    def mask(n, device, position, stride):
        owner = (device == iota((n, ROWS), 1)).astype(BF16)
        head = first_head + jnp.minimum(iota((n, ROWS), 1), 1)
        position = position * stride + head % stride
        alive = position.astype(F32) < dot(owner, counts, MINOR)
        return jnp.where(alive, 0.0, NEG).astype(BF16)

    def in_half(f, b):
        return SEG * (zh + f - 2 * zh * f) + b

    r = iota((512, ROWS), 0)
    device = (x * NY + (y ^ (r >> 8))) * NZ + in_half((r >> 7) & 1, (r >> 5) & 3)
    MKM[...] = mask(512, device, r & 31, 4)
    r = iota((1024, ROWS), 0)
    device = ((x + NX - ((r >> 7) & 3)) & 3) * NY + ((y + NY - ((r >> 5) & 3)) & 3)
    MKL[...] = mask(1024, device * NZ + in_half(r >> 9, (r >> 3) & 3), r & 7, 16)
    in_m01.wait_recv()
    in_m11 = middle(1, 1, HM.at[0, 1], partner)

    for o in order:
        in_near[o].wait_recv()
    absorb(
        GF[:, :, 0, 0:LONG].reshape(512, ROWS),
        GF[:, :, 0, LONG:].reshape(512, ROWS),
        MKL[0:512],
    )
    in_m10.wait_recv()
    middles = [HM[0, 0], HM[0, 1], HM[1, 0]]
    absorb(
        jnp.concatenate([part[0:ROWS] for part in middles], axis=0),
        jnp.concatenate([part[ROWS:] for part in middles], axis=0),
        MKM[0:384],
    )
    backs = []
    alive_lanes = [
        (iota((1, ROWS), 1).astype(F32) < SRC[b][1:2]).astype(F32) for b in range(SEG)
    ]

    def give_back(b):
        halves = []
        for h in range(2):
            cols = slice(h * ROWS, (h + 1) * ROWS)
            scale = alive_lanes[b] / L[b][0:1, cols]
            halves.append(O[b][h * 64 : (h + 1) * 64, cols] * scale)
        AS[b] = jnp.concatenate(halves, axis=0).astype(BF16)
        target = b + zh * (SEG - 1 - 2 * b)
        here = (place == 1) | (place == 2)
        here = here | ((place == 0) & (target == 1)) | ((place == 3) & (target == 2))
        here = here & (place != target)
        copy = remote(AS.at[b], AT.at[pair], at_s.at[b], at_r.at[pair], at(x, y, SEG * zh + b))
        backs.append((copy, here))
        pl.when(here)(copy.start)

    for dx in (0, 2):
        for o in order:
            if o // NY in (dx, dx + 1):
                in_other[o].wait_recv()
        keys = GF[dx : dx + 2, :, 1, 0:LONG].reshape(256, ROWS)
        values = GF[dx : dx + 2, :, 1, LONG:].reshape(256, ROWS)
        masks = MKL[512 + 128 * dx : 768 + 128 * dx]
        if dx:
            in_m11.wait_recv()
            keys = jnp.concatenate([keys, HM[1, 1, 0:ROWS]], axis=0)
            values = jnp.concatenate([values, HM[1, 1, ROWS:]], axis=0)
            masks = jnp.concatenate([masks, MKM[384:]], axis=0)
        absorb(keys, values, masks, give_back if dx else None)
    AT[pair] = AS[zj]
    for copy in pending:
        copy.wait_send()
    mine = pl.ds(pl.multiple_of(core * HALF, HALF), HALF)
    other = pl.ds(pl.multiple_of((1 - core) * HALF, HALF), HALF)
    groups = [slice(g * ROWS, (g + 1) * ROWS) for g in range(3)]
    for_other = jnp.zeros((ROWS, HALF), F32)
    for g in range(3):
        arrival = remote(AS.at[0], AT.at[g], at_s.at[0], at_r.at[g], sibling)
        pl.when(pair != g)(arrival.wait_recv)
        for_other = for_other + dot(AT[g], w_out[groups[g], other], MAJOR)
    PO[...] = for_other.astype(BF16)
    in_o = remote(PO, other_part, o_s.at[0], o_r.at[0], sibling)
    in_o.start()
    OWN[...] = dot(AT[...].reshape(HALF, ROWS), w_out[:, mine], MAJOR)
    hand_out = pltpu.make_async_copy(OWN, own_part, loc_sem.at[0])
    hand_out.start()
    hand_out.wait()
    for copy, here in backs:
        pl.when(here)(copy.wait_send)
    in_o.wait()


def shards(tiles, ln_gain, w_qkv, w_out, tile_source, tissue_count):
    dma = pltpu.SemaphoreType.DMA
    scratch = [
        pltpu.VMEM((D, 3 * ROWS), BF16),
        pltpu.VMEM((HALF, D), BF16),
        pltpu.VMEM((6, ROWS), F32),
        pltpu.VMEM((1, ROWS), jnp.int32),
        pltpu.SMEM((1,), jnp.int32),
        pltpu.VMEM((NX, 32, HALF), BF16),
        pltpu.VMEM((NX, 32, HALF), BF16),
        pltpu.VMEM((2 * NY, 16, HALF), BF16),
        pltpu.VMEM((NY, NZ, 16, HALF), BF16),
        pltpu.VMEM((NY, NZ, 16, HALF), BF16),
        pltpu.VMEM((SEG, 8, ROWS), F32),
        pltpu.VMEM((512, 3 * ROWS), BF16),
        pltpu.VMEM((512, 512), BF16),
        pltpu.VMEM((2, 160, 512), BF16),
        pltpu.VMEM((512, ROWS), BF16),
        pltpu.VMEM((512, ROWS), BF16),
        pltpu.VMEM((512, ROWS), BF16),
        pltpu.VMEM((512, ROWS), BF16),
        pltpu.VMEM((1024, ROWS), BF16),
        pltpu.VMEM((NX, 8, ROWS), F32),
        pltpu.VMEM((NY, 8, ROWS), F32),
        pltpu.VMEM((NZ, 8, ROWS), F32),
        pltpu.VMEM((NX, NY, 2, 64, ROWS), BF16),
        pltpu.VMEM((2, 2, 256, ROWS), BF16),
        pltpu.VMEM((SEG, 256, 256), BF16),
        pltpu.VMEM((SEG, 8, 256), F32),
        pltpu.VMEM((SEG, 8, 256), F32),
        pltpu.VMEM((SEG, ROWS, 256), F32),
        pltpu.VMEM((SEG, ROWS, ROWS), BF16),
        pltpu.VMEM((3, ROWS, ROWS), BF16),
        pltpu.VMEM((ROWS, HALF), BF16),
        pltpu.VMEM((ROWS, HALF), F32),
        dma((5,)), dma((3,)), pltpu.SemaphoreType.REGULAR,
    ]
    for size in (NX, NY * NZ, NY, SEG, NX * NY * 2, 4, SEG, 1, NX, NY, NZ):
        scratch += [dma((size,)), dma((size,))]
    anywhere = pl.BlockSpec(memory_space=pltpu.HBM)
    own_part, other_part = pl.pallas_call(
        kernel,
        out_shape=(
            jax.ShapeDtypeStruct((ROWS, HALF), F32),
            jax.ShapeDtypeStruct((ROWS, HALF), BF16),
        ),
        in_specs=[anywhere] * 6,
        out_specs=(anywhere, anywhere),
        scratch_shapes=scratch,
        compiler_params=pltpu.CompilerParams(
            collective_id=0, has_side_effects=True, vmem_limit_bytes=64 << 20
        ),
    )(
        tiles.reshape(NX, 32, HALF),
        ln_gain.reshape(6, ROWS),
        jnp.transpose(w_qkv, (1, 0, 2)),
        w_out,
        tile_source.reshape(1, ROWS),
        tissue_count,
    )
    return (own_part + other_part.astype(F32)).astype(BF16)


def solution(mesh):
    return jax.shard_map(
        shards,
        mesh=mesh,
        in_specs=(
            P("seq", "head"),
            P(),
            P(None, None, "head"),
            P("head", None),
            P("seq"),
            P("seq"),
        ),
        out_specs=P("seq", "head"),
        check_vma=False,
    )
```

```python
import jax
import jax.numpy as jnp
from jax import lax
from jax.experimental import pallas as pl
from jax.experimental.pallas import tpu as pltpu
from jax.sharding import PartitionSpec as P

D = 768
HALF = 384
ROWS = 128
NX, NY, NZ = 4, 4, 8
SEG = 4
LONG = SEG * 8
NEG = -1e30
F32 = jnp.float32
BF16 = jnp.bfloat16
MESH = pl.DeviceIdType.MESH
PLAIN = (((1,), (0,)), ((), ()))
MINOR = (((1,), (1,)), ((), ()))
MAJOR = (((0,), (0,)), ((), ()))


def iota(shape, dim):
    return lax.broadcasted_iota(jnp.int32, shape, dim)


def dot(a, b, dims):
    return lax.dot_general(a, b, dims, preferred_element_type=F32)


def kernel(
    tiles, gain_in, w_qkv, w_out_in, src_in, cnt_in,
    own_part, other_part,
    w_v, w_out, gain, src, cnt, T, A, C, DD, E, SRC, R, PM, SEL,
    KS, VS, MKS, MKM, MKL, CX, CY, CZ, GF, HM, QA, M, L, O, AS, AT, PO, OWN,
    w_sem, loc_sem, ready,
    xs_s, xs_r, zs_s, zs_r, ps_s, ps_r, src_s, src_r,
    gf_s, gf_r, hm_s, hm_r, at_s, at_r, o_s, o_r,
    cx_s, cx_r, cy_s, cy_r, cz_s, cz_r,
):
    seq = lax.axis_index("seq")
    core = lax.axis_index("head")
    x, y, z = seq // (NY * NZ), (seq // NZ) % NY, seq % NZ
    zh, zj = z // SEG, z % SEG
    place = zj + zh * (SEG - 1 - 2 * zj)
    pair = place % 3
    first_head = 6 * core + 2 * pair
    sibling = {"head": 1 - core}
    pending = []

    def at(px, py, pz):
        return {"seq": (px * NY + py) * NZ + pz}

    def remote(source, target, s_sem, r_sem, device):
        return pltpu.make_async_remote_copy(
            src_ref=source, dst_ref=target, send_sem=s_sem, recv_sem=r_sem,
            device_id=device, device_id_type=MESH,
        )

    def send(source, target, s_sem, r_sem, device):
        copy = remote(source, target, s_sem, r_sem, device)
        copy.start()
        pending.append(copy)
        return copy

    lanes = pl.ds(pl.multiple_of(pair * ROWS, ROWS), ROWS)
    weights = [
        pltpu.make_async_copy(w_qkv.at[t, :, lanes], w_v.at[:, t * ROWS : (t + 1) * ROWS], w_sem.at[t])
        for t in range(3)
    ]
    weights += [pltpu.make_async_copy(w_out_in, w_out, w_sem.at[3])]
    weights += [pltpu.make_async_copy(gain_in, gain, w_sem.at[4])]
    small = [
        pltpu.make_async_copy(src_in, src, loc_sem.at[1]),
        pltpu.make_async_copy(cnt_in, cnt, loc_sem.at[2]),
    ]
    own_t = pltpu.make_async_copy(tiles, T, loc_sem.at[0])
    barrier = pltpu.get_barrier_semaphore()
    peers = [at((x + k) % NX, y, z) for k in range(1, NX)] + [sibling]
    plane = [(dy, dz) for dy in (2, 1, 3, 0) for dz in (4, 3, 5, 2, 6, 1, 7, 0) if dy or dz]
    y_peers = [at(x, (y + k) % NY, z) for k in range(1, NY)]
    peers += y_peers + [at(x, y, (z + k) % NZ) for k in range(1, NZ)]
    for peer in peers:
        pl.semaphore_signal(barrier, inc=1, device_id=peer, device_id_type=MESH)
    for copy in small + [own_t] + weights:
        copy.start()
    own_t.wait()
    pl.semaphore_wait(barrier, len(peers))

    in_x = [
        send(T.at[(x + k) % NX], A.at[k], xs_s.at[k], xs_r.at[k], at((x + k) % NX, y, z))
        for k in range(1, NX)
    ]
    for copy in small:
        copy.wait()
    own_count = cnt[0]
    rows8 = iota((8, ROWS), 0)
    tag = jnp.where(rows8 == 0, src[...] // ROWS, own_count)
    SRC[zj] = tag.astype(F32)
    CX[0] = jnp.where(iota((8, ROWS), 1) == seq, own_count, 0).astype(F32)
    for peer in y_peers:
        pl.semaphore_signal(ready, inc=1, device_id=peer, device_id_type=MESH)
    in_cx = [
        send(CX.at[0], CX.at[k], cx_s.at[k], cx_r.at[k], at((x + k) % NX, y, z))
        for k in range(1, NX)
    ]
    in_src = [
        send(SRC.at[zj], SRC.at[zj], src_s.at[t], src_r.at[t], at(x, y, SEG * zh + (zj + t) % SEG))
        for t in range(1, SEG)
    ]
    A[0] = T[x]
    row, col = iota((ROWS, ROWS), 0), iota((ROWS, ROWS), 1)
    turn = (((row >> 2) & 3) * 32 + (row >> 4) * 4 + (row & 3) == col).astype(BF16)
    for copy in in_x:
        copy.wait_recv()
    pl.semaphore_wait(ready, len(y_peers))
    turned = dot(turn, A[...].reshape(ROWS, HALF), PLAIN)
    C[...] = turned.astype(BF16).reshape(2 * NY, 16, HALF)

    in_z = [[] for _ in range(NY)]
    for dy, dz in plane:
        yt, zt = (y + dy) % NY, (z + dz) % NZ
        o = dy * NZ + dz
        in_z[dy].append(
            send(C.at[2 * yt + zt // SEG], DD.at[dy, dz], zs_s.at[o], zs_r.at[o], at(x, yt, zt))
        )
    DD[0, 0] = C[2 * y + zh]
    for copy in in_cx:
        copy.wait_recv()
    CY[0] = jnp.sum(CX[...], axis=0)
    in_cy = [send(CY.at[0], CY.at[k], cy_s.at[k], cy_r.at[k], y_peers[k - 1]) for k in range(1, NY)]

    for copy in in_src:
        copy.wait_recv()
    lane512 = iota((1, 512), 1)
    from_x, from_y = (x + NX - ((lane512 >> 2) & 3)) & 3, (y + NY - (lane512 >> 7)) & 3
    from_z = (z + NZ - ((lane512 >> 4) & 7)) & 7
    code = (((from_x * NY + from_y) * NZ + from_z) * SEG + (lane512 & 3)).astype(F32)
    place_iota = iota((ROWS, ROWS), 0).astype(F32)
    for b in range(SEG):
        block = SRC[b]
        wanted = jnp.transpose(block)[:, 0:1] * SEG + b
        PM[b * ROWS : (b + 1) * ROWS] = (wanted == code).astype(BF16)
        alive = place_iota < block[1:2]
        MKS[b * ROWS : (b + 1) * ROWS] = jnp.where(alive, 0.0, NEG).astype(BF16)
        QA[b, 0:ROWS, ROWS:] = (col == 0).astype(BF16)
        QA[b, ROWS:, ROWS:] = (col == 1).astype(BF16)
        M[b] = jnp.full((8, 256), NEG, F32)
        L[b] = jnp.zeros((8, 256), F32)
        O[b] = jnp.zeros((ROWS, 256), F32)
    out_row, from_row = iota((160, 512), 0), iota((160, 512), 1)
    for h in range(2):
        head = first_head + h
        mid = (out_row >> 5) * ROWS + (out_row & 31) * 4 + head % 4
        far_row = out_row - ROWS
        far = (far_row >> 3) * ROWS + (far_row & 7) * 16 + head
        select = (jnp.where(out_row < ROWS, mid, far) == from_row).astype(BF16)
        SEL[h] = dot(select, PM[...], PLAIN).astype(BF16)
    for copy in weights:
        copy.wait()

    gain_mine = jnp.concatenate([gain[pl.ds(3 * core + i, 1)] for i in range(3)], axis=1)
    gain_other = jnp.concatenate([gain[pl.ds(3 - 3 * core + i, 1)] for i in range(3)], axis=1)
    w_mine = w_v[pl.ds(pl.multiple_of(core * HALF, HALF), HALF)]
    w_other = w_v[pl.ds(pl.multiple_of((1 - core) * HALF, HALF), HALF)]

    def project(c):
        a = DD[c].reshape(ROWS, HALF).astype(F32)
        b = E[c].reshape(ROWS, HALF).astype(F32)
        mean = (jnp.sum(a, 1, keepdims=True) + jnp.sum(b, 1, keepdims=True)) / D
        a, b = a - mean, b - mean
        var = (jnp.sum(a * a, 1, keepdims=True) + jnp.sum(b * b, 1, keepdims=True)) / D
        scale = lax.rsqrt(var + 1e-05)
        a = (a * scale * gain_mine).astype(BF16)
        b = (b * scale * gain_other).astype(BF16)
        R[c * ROWS : (c + 1) * ROWS] = (dot(a, w_mine, PLAIN) + dot(b, w_other, PLAIN)).astype(BF16)

    turns = (2, 1, 3, 0)
    in_p = {}
    for i, c in enumerate(turns):
        for copy in in_z[c]:
            copy.wait_recv()
        in_p[c] = send(DD.at[c], E.at[c], ps_s.at[c], ps_r.at[c], sibling)
        if i:
            in_p[turns[i - 1]].wait_recv()
            project(turns[i - 1])
        if i == 1:
            for copy in in_cy:
                copy.wait_recv()
            CZ[0] = jnp.sum(CY[...], axis=0)
            in_cz = [
                send(CZ.at[0], CZ.at[k], cz_s.at[k], cz_r.at[k], at(x, y, (z + k) % NZ))
                for k in range(1, NZ)
            ]
    in_p[turns[-1]].wait_recv()
    project(turns[-1])

    low = (iota((1, 2 * ROWS), 1) & 127) < 64
    kv = R[:, ROWS:]
    picked = jnp.where(low, dot(SEL[0], kv, PLAIN), dot(SEL[1], kv, PLAIN)).astype(BF16)
    HM[0, 0, 0:ROWS] = picked[0:ROWS, 0:ROWS]
    HM[0, 0, ROWS:] = picked[0:ROWS, ROWS:]
    GF[0, 0, 0, 0:LONG] = picked[ROWS:, 0:ROWS]
    GF[0, 0, 0, LONG : 2 * LONG] = picked[ROWS:, ROWS:]

    def to_xy(f, o):
        dx, dy = o // NY, o % NY
        return send(
            GF.at[0, 0, f], GF.at[dx, dy, f], gf_s.at[2 * o + f], gf_r.at[2 * o + f],
            at((x + dx) % NX, (y + dy) % NY, z),
        )

    def middle(yy, f, source, device):
        o = 2 * yy + f
        return send(source, HM.at[yy, f], hm_s.at[o], hm_r.at[o], device)

    mirror, partner = at(x, y, NZ - 1 - z), at(x, y + 1 - 2 * (y % 2), z)
    order = (10, 6, 14, 2, 9, 11, 8, 5, 7, 13, 15, 1, 3, 4, 12)
    in_far = send(GF.at[0, 0, 0], GF.at[0, 0, 1], gf_s.at[1], gf_r.at[1], mirror)
    in_m01 = middle(0, 1, HM.at[0, 0], mirror)
    in_near = {o: to_xy(0, o) for o in order}
    in_m10 = middle(1, 0, HM.at[0, 0], partner)
    qkv = dot(PM[...], R[...], PLAIN)
    KS[...] = qkv[:, ROWS : 2 * ROWS].astype(BF16)
    VS[...] = qkv[:, 2 * ROWS :].astype(BF16)
    q32 = qkv[:, 0:ROWS].astype(BF16).astype(F32) * 0.125
    for b in range(SEG):
        q_b = q32[b * ROWS : (b + 1) * ROWS]
        QA[b, 0:ROWS, 0:ROWS] = jnp.where(col < 64, q_b, 0.0).astype(BF16)
        QA[b, ROWS:, 0:ROWS] = jnp.where(col < 64, 0.0, q_b).astype(BF16)

    def absorb(keys, values, masks, finish=None):
        keys = jnp.concatenate([keys, masks], axis=1)
        turned_values = jnp.transpose(values)
        blocks = range(SEG)
        scores = [dot(keys, QA[b], MINOR) for b in blocks]
        old = [M[b][0:1] for b in blocks]
        new = [jnp.maximum(old[b], jnp.max(scores[b], axis=0, keepdims=True)) for b in blocks]
        weight = [jnp.exp(scores[b] - new[b]) for b in blocks]
        rescale = [jnp.exp(old[b] - new[b]) for b in blocks]
        mixed = [dot(turned_values, weight[b].astype(BF16), PLAIN) for b in blocks]
        for b in blocks:
            total = L[b][0:1] * rescale[b] + jnp.sum(weight[b], axis=0, keepdims=True)
            O[b] = O[b] * rescale[b] + mixed[b]
            M[b] = jnp.broadcast_to(new[b], (8, 256))
            L[b] = jnp.broadcast_to(total, (8, 256))
            if finish is not None:
                finish(b)

    absorb(KS[...], VS[...], MKS[...])
    in_far.wait_recv()
    in_other = {o: to_xy(1, o) for o in order}
    for copy in in_cz:
        copy.wait_recv()
    counts = jnp.broadcast_to(jnp.sum(CZ[...], axis=0)[0:1], (ROWS, ROWS)).astype(BF16)

    def mask(n, device, position, stride):
        owner = (device == iota((n, ROWS), 1)).astype(BF16)
        head = first_head + jnp.minimum(iota((n, ROWS), 1), 1)
        position = position * stride + head % stride
        alive = position.astype(F32) < dot(owner, counts, MINOR)
        return jnp.where(alive, 0.0, NEG).astype(BF16)

    def in_half(f, b):
        return SEG * (zh + f - 2 * zh * f) + b

    r = iota((512, ROWS), 0)
    device = (x * NY + (y ^ (r >> 8))) * NZ + in_half((r >> 7) & 1, (r >> 5) & 3)
    MKM[...] = mask(512, device, r & 31, 4)
    r = iota((1024, ROWS), 0)
    device = ((x + NX - ((r >> 7) & 3)) & 3) * NY + ((y + NY - ((r >> 5) & 3)) & 3)
    MKL[...] = mask(1024, device * NZ + in_half(r >> 9, (r >> 3) & 3), r & 7, 16)
    in_m01.wait_recv()
    in_m11 = middle(1, 1, HM.at[0, 1], partner)

    for o in order:
        in_near[o].wait_recv()
    absorb(
        GF[:, :, 0, 0:LONG].reshape(512, ROWS),
        GF[:, :, 0, LONG:].reshape(512, ROWS),
        MKL[0:512],
    )
    in_m10.wait_recv()
    middles = [HM[0, 0], HM[0, 1], HM[1, 0]]
    absorb(
        jnp.concatenate([part[0:ROWS] for part in middles], axis=0),
        jnp.concatenate([part[ROWS:] for part in middles], axis=0),
        MKM[0:384],
    )
    backs = []
    alive_lanes = [
        (iota((1, ROWS), 1).astype(F32) < SRC[b][1:2]).astype(F32) for b in range(SEG)
    ]

    def give_back(b):
        halves = []
        for h in range(2):
            cols = slice(h * ROWS, (h + 1) * ROWS)
            scale = alive_lanes[b] / L[b][0:1, cols]
            halves.append(O[b][h * 64 : (h + 1) * 64, cols] * scale)
        AS[b] = jnp.concatenate(halves, axis=0).astype(BF16)
        target = b + zh * (SEG - 1 - 2 * b)
        here = (place == 1) | (place == 2)
        here = here | ((place == 0) & (target == 1)) | ((place == 3) & (target == 2))
        here = here & (place != target)
        copy = remote(AS.at[b], AT.at[pair], at_s.at[b], at_r.at[pair], at(x, y, SEG * zh + b))
        backs.append((copy, here))
        pl.when(here)(copy.start)

    for dx in (0, 2):
        for o in order:
            if o // NY in (dx, dx + 1):
                in_other[o].wait_recv()
        keys = GF[dx : dx + 2, :, 1, 0:LONG].reshape(256, ROWS)
        values = GF[dx : dx + 2, :, 1, LONG:].reshape(256, ROWS)
        masks = MKL[512 + 128 * dx : 768 + 128 * dx]
        if dx:
            in_m11.wait_recv()
            keys = jnp.concatenate([keys, HM[1, 1, 0:ROWS]], axis=0)
            values = jnp.concatenate([values, HM[1, 1, ROWS:]], axis=0)
            masks = jnp.concatenate([masks, MKM[384:]], axis=0)
        absorb(keys, values, masks, give_back if dx else None)
    AT[pair] = AS[zj]
    for copy in pending:
        copy.wait_send()
    mine = pl.ds(pl.multiple_of(core * HALF, HALF), HALF)
    other = pl.ds(pl.multiple_of((1 - core) * HALF, HALF), HALF)
    groups = [slice(g * ROWS, (g + 1) * ROWS) for g in range(3)]
    for_other = jnp.zeros((ROWS, HALF), F32)
    for g in range(3):
        arrival = remote(AS.at[0], AT.at[g], at_s.at[0], at_r.at[g], sibling)
        pl.when(pair != g)(arrival.wait_recv)
        for_other = for_other + dot(AT[g], w_out[groups[g], other], MAJOR)
    PO[...] = for_other.astype(BF16)
    in_o = remote(PO, other_part, o_s.at[0], o_r.at[0], sibling)
    in_o.start()
    OWN[...] = dot(AT[...].reshape(HALF, ROWS), w_out[:, mine], MAJOR)
    hand_out = pltpu.make_async_copy(OWN, own_part, loc_sem.at[0])
    hand_out.start()
    hand_out.wait()
    for copy, here in backs:
        pl.when(here)(copy.wait_send)
    in_o.wait()


def shards(tiles, ln_gain, w_qkv, w_out, tile_source, tissue_count):
    dma = pltpu.SemaphoreType.DMA
    scratch = [
        pltpu.VMEM((D, 3 * ROWS), BF16),
        pltpu.VMEM((HALF, D), BF16),
        pltpu.VMEM((6, ROWS), F32),
        pltpu.VMEM((1, ROWS), jnp.int32),
        pltpu.SMEM((1,), jnp.int32),
        pltpu.VMEM((NX, 32, HALF), BF16),
        pltpu.VMEM((NX, 32, HALF), BF16),
        pltpu.VMEM((2 * NY, 16, HALF), BF16),
        pltpu.VMEM((NY, NZ, 16, HALF), BF16),
        pltpu.VMEM((NY, NZ, 16, HALF), BF16),
        pltpu.VMEM((SEG, 8, ROWS), F32),
        pltpu.VMEM((512, 3 * ROWS), BF16),
        pltpu.VMEM((512, 512), BF16),
        pltpu.VMEM((2, 160, 512), BF16),
        pltpu.VMEM((512, ROWS), BF16),
        pltpu.VMEM((512, ROWS), BF16),
        pltpu.VMEM((512, ROWS), BF16),
        pltpu.VMEM((512, ROWS), BF16),
        pltpu.VMEM((1024, ROWS), BF16),
        pltpu.VMEM((NX, 8, ROWS), F32),
        pltpu.VMEM((NY, 8, ROWS), F32),
        pltpu.VMEM((NZ, 8, ROWS), F32),
        pltpu.VMEM((NX, NY, 2, 64, ROWS), BF16),
        pltpu.VMEM((2, 2, 256, ROWS), BF16),
        pltpu.VMEM((SEG, 256, 256), BF16),
        pltpu.VMEM((SEG, 8, 256), F32),
        pltpu.VMEM((SEG, 8, 256), F32),
        pltpu.VMEM((SEG, ROWS, 256), F32),
        pltpu.VMEM((SEG, ROWS, ROWS), BF16),
        pltpu.VMEM((3, ROWS, ROWS), BF16),
        pltpu.VMEM((ROWS, HALF), BF16),
        pltpu.VMEM((ROWS, HALF), F32),
        dma((5,)), dma((3,)), pltpu.SemaphoreType.REGULAR,
    ]
    for size in (NX, NY * NZ, NY, SEG, NX * NY * 2, 4, SEG, 1, NX, NY, NZ):
        scratch += [dma((size,)), dma((size,))]
    anywhere = pl.BlockSpec(memory_space=pltpu.HBM)
    own_part, other_part = pl.pallas_call(
        kernel,
        out_shape=(
            jax.ShapeDtypeStruct((ROWS, HALF), F32),
            jax.ShapeDtypeStruct((ROWS, HALF), BF16),
        ),
        in_specs=[anywhere] * 6,
        out_specs=(anywhere, anywhere),
        scratch_shapes=scratch,
        compiler_params=pltpu.CompilerParams(
            collective_id=0, has_side_effects=True, vmem_limit_bytes=64 << 20
        ),
    )(
        tiles.reshape(NX, 32, HALF),
        ln_gain.reshape(6, ROWS),
        jnp.transpose(w_qkv, (1, 0, 2)),
        w_out,
        tile_source.reshape(1, ROWS),
        tissue_count,
    )
    return (own_part + other_part.astype(F32)).astype(BF16)


def solution(mesh):
    return jax.shard_map(
        shards,
        mesh=mesh,
        in_specs=(
            P("seq", "head"),
            P(),
            P(None, None, "head"),
            P("head", None),
            P("seq"),
            P("seq"),
        ),
        out_specs=P("seq", "head"),
        check_vma=False,
    )
```
